512 devices in a mesh: seq: 64 (over x, z, core), head: 8 (over y).
Axes of the slice: x: 4, y: 8, z: 8, core: 2. Of those that a mesh axis runs over, the one named last changes fastest.
Arguments:
- query_tokens: bfloat16 [2, 32768, 4096], P(None, 'seq', 'head'), may hold values from -6 to 6
- key_tokens: bfloat16 [2, 32768, 4096], P(None, 'seq', 'head'), may hold values from -16 to 16
- value_tokens: bfloat16 [2, 32768, 4096], P(None, 'seq', 'head'), may hold values from -16 to 16
- token_rates: float32 [3, 2, 16, 32768], P(None, None, 'head', 'seq'), may hold values from 0.1 to 1
- fast_init: bfloat16 [3, 16, 256, 256], P(None, 'head'), may hold values from -0.375 to 0.375
Outputs:
- mixer_out: bfloat16 [2, 32768, 4096], P(None, ('seq', 'head'))
The draws below stay inside these ranges and needn't reach their ends.
All inputs are finite; a program needn't handle non-finite values.
Results may differ from the reference program's by a relative error of at most 0.017.
Values may be sent and summed in bfloat16 or wider, within the bound.
No kernel may reach another device: no remote copies, remote signals or barrier semaphores. Data moves between devices by JAX's collectives and lax.ppermute only.
A program may use at most 64 MiB of HBM per device.

```python
import math
import jax
import jax.numpy as jnp
from jax import lax

HD = 256
GROUPS = 2
HEADS = 16
GROUP = 32768


def feature_draw(key, salt):
    full_shape = (GROUPS, GROUP, HEADS * HD)
    key_scale, key_base = jax.random.split(jax.random.fold_in(key, salt), 2)
    scales = jnp.exp(jax.random.uniform(key_scale, (full_shape[-1],), jnp.float32, jnp.log(0.4), jnp.log(4.0)))
    result = jnp.clip(jax.random.normal(key_base, full_shape, jnp.float32), -4.0, 4.0) * scales
    return result.astype(jnp.bfloat16)


def draw_key_tokens(key, part):
    return feature_draw(key, 11)


def draw_value_tokens(key, part):
    return feature_draw(key, 23)


def levels(stream_key, extent, cuts, low, high):
    level, own = 1.0, jax.random.fold_in(stream_key, 6)
    for dim, shards_of in cuts:
        heights = jnp.exp(jax.random.uniform(jax.random.fold_in(own, dim), (shards_of,), jnp.float32, low / len(cuts), high / len(cuts)))
        level = level * jnp.repeat(heights, extent[dim] // shards_of).reshape([-1 if axis == dim else 1 for axis in range(len(extent))])
    return level


def bell_draw(rng, extent, spread, limit, cuts=(), kind=jnp.bfloat16):
    gain = levels(rng, extent, cuts, -0.22, 0.18) if cuts else 1.0
    values = jax.random.normal(rng, extent, jnp.float32) * spread * gain
    return jnp.minimum(jnp.maximum(values, -limit), limit).astype(kind)


def setup_inputs(seed: int = 0) -> dict:
    keys = jax.random.split(jax.random.key(seed), 6)
    query_tokens = bell_draw(keys[0], (GROUPS, GROUP, HEADS * HD), 1.0, 6.0, ((1, 64), (2, 8)))
    key_tokens = draw_key_tokens(jax.random.fold_in(keys[5], 71), 0)
    value_tokens = draw_value_tokens(jax.random.fold_in(keys[5], 71), 0)
    token_rates = jnp.clip(jnp.exp(math.log(1.0) - 2.3025851 * jax.random.uniform(keys[3], (3, GROUPS, HEADS, GROUP), jnp.float32) ** levels(keys[3], (3, GROUPS, HEADS, GROUP), ((2, 8), (3, 64)), -0.2, 0.2)), 0.1, 1.0)
    fast_init = bell_draw(keys[4], (3, HEADS, HD, HD), HD ** -0.5, 0.375, ((1, 8),))
    return dict(query_tokens=query_tokens, key_tokens=key_tokens, value_tokens=value_tokens, token_rates=token_rates, fast_init=fast_init)


step_size = 0.05
eps_grad = 1e-05
eps_row = 1e-06

def one_head(inputs):
    query_rows, key_rows, value_rows, rate_rows, weight_init = inputs
    fast_state = weight_init.astype(jnp.float32)
    target = jnp.sqrt(lax.optimization_barrier(jnp.mean(fast_state * fast_state, axis=-1, keepdims=True)))
    results = []
    for block_index in range(GROUPS):
        keys_now = key_rows[block_index]
        values_now = value_rows[block_index]
        current = fast_state.astype(jnp.bfloat16)
        gate_proj = jnp.dot(keys_now, current[0], preferred_element_type=jnp.float32)
        up_proj = jnp.dot(keys_now, current[1], preferred_element_type=jnp.float32)
        sigmoid_gate = jax.nn.sigmoid(gate_proj)
        silu_gate = gate_proj * sigmoid_gate
        hidden = (silu_gate * up_proj).astype(jnp.bfloat16)
        scaled_hidden = (hidden.astype(jnp.float32) * rate_rows[2, block_index][:, None]).astype(jnp.bfloat16)
        grad_down = -jnp.dot(scaled_hidden.T, values_now, preferred_element_type=jnp.float32)
        hidden_grad = -jnp.dot(values_now, current[2].T, preferred_element_type=jnp.float32)
        gate_grad = hidden_grad * up_proj * sigmoid_gate * (1.0 + gate_proj * (1.0 - sigmoid_gate))
        up_grad = hidden_grad * silu_gate
        gate_scaled = (gate_grad * rate_rows[0, block_index][:, None]).astype(jnp.bfloat16)
        up_scaled = (up_grad * rate_rows[1, block_index][:, None]).astype(jnp.bfloat16)
        grad_gate = jnp.dot(keys_now.T, gate_scaled, preferred_element_type=jnp.float32)
        grad_up = jnp.dot(keys_now.T, up_scaled, preferred_element_type=jnp.float32)
        gradients_now = jnp.stack([grad_gate, grad_up, grad_down])
        grad_rms = jnp.sqrt(lax.optimization_barrier(jnp.mean(gradients_now * gradients_now, axis=(1, 2), keepdims=True)) + eps_grad)
        stepped = fast_state - step_size * gradients_now / grad_rms
        fast_state = stepped * target * lax.rsqrt(lax.optimization_barrier(jnp.mean(stepped * stepped, axis=-1, keepdims=True)) + eps_row)
        applied = fast_state.astype(jnp.bfloat16)
        query_now = query_rows[block_index]
        gate_query = jnp.dot(query_now, applied[0], preferred_element_type=jnp.float32)
        up_query = jnp.dot(query_now, applied[1], preferred_element_type=jnp.float32)
        hidden_query = (gate_query * jax.nn.sigmoid(gate_query) * up_query).astype(jnp.bfloat16)
        results.append(jnp.dot(hidden_query, applied[2], preferred_element_type=jnp.float32).astype(jnp.bfloat16))
    return jnp.stack(results)

def reference(query_tokens, key_tokens, value_tokens, token_rates, fast_init):

    def per_head(array):
        return array.reshape(GROUPS, GROUP, HEADS, HD).transpose(2, 0, 1, 3)
    per_head_out = lax.map(one_head, (per_head(query_tokens), per_head(key_tokens), per_head(value_tokens), token_rates.transpose(2, 0, 1, 3), fast_init.transpose(1, 0, 2, 3)))
    return per_head_out.transpose(1, 2, 0, 3).reshape(GROUPS, GROUP, HEADS * HD)
```

```python
import jax
import jax.numpy as jnp
from jax import lax
from jax.experimental import pallas as pl
from jax.experimental.pallas import tpu as pltpu
from jax.sharding import Mesh, PartitionSpec as P

step_size = 0.05
eps_grad = 1e-05
eps_row = 1e-06
f32 = jnp.float32
bf16 = jnp.bfloat16
NT = (((1,), (1,)), ((), ()))
NN = (((1,), (0,)), ((), ()))


def dot(a, b, dims):
    return lax.dot_general(a, b, dims, preferred_element_type=f32)


def head_init(init_ref):
    return [
        jnp.transpose(init_ref[0, 0].astype(f32)),
        jnp.transpose(init_ref[1, 0].astype(f32)),
        init_ref[2, 0].astype(f32),
    ]


def row_mean(w, i):
    return jnp.mean(w * w, axis=1 if i == 2 else 0, keepdims=True)


def half_gradients(keys, values, rate_gate, rate_up, rate_down, w_gate, w_up, w_down):
    gate = dot(w_gate, keys, NT)
    up = dot(w_up, keys, NT)
    err = dot(w_down, values, NT)
    sig = jax.nn.sigmoid(gate)
    silu = gate * sig
    hidden = (silu * up).astype(bf16)
    scaled = (hidden.astype(f32) * rate_down).astype(bf16)
    gate_grad = err * up * sig * (1.0 + gate * (1.0 - sig))
    gate_scaled = (gate_grad * rate_gate).astype(bf16)
    up_scaled = (err * silu * rate_up).astype(bf16)
    return (
        dot(gate_scaled, keys, NN),
        dot(up_scaled, keys, NN),
        dot(scaled, values, NN),
    )


def all_gradients(c, block, weights, k_ref, v_ref, kv_ref, rates_ref, rates_other_ref, out_ref):
    own = half_gradients(
        k_ref[0], v_ref[0], *[rates_ref[i, block, pl.ds(c, 1), :] for i in (0, 1, 2)], *weights
    )
    other = half_gradients(
        kv_ref[0], kv_ref[1], *[rates_other_ref[i, block : block + 1, :] for i in (0, 1, 2)], *weights
    )
    for i in range(3):
        out_ref[256 * i : 256 * (i + 1), :] = (own[i] + other[i]).astype(bf16)


def updated(state, init, grad_ref):
    result = []
    for i in range(3):
        grad = grad_ref[256 * i : 256 * (i + 1), :].astype(f32)
        rms = jnp.sqrt(jnp.mean(grad * grad, keepdims=True) + eps_grad)
        stepped = state[i] + grad * (step_size / rms)
        target = jnp.sqrt(row_mean(init[i], i))
        result.append(stepped * (target * lax.rsqrt(row_mean(stepped, i) + eps_row)))
    return result


def first_kernel(c_ref, init_ref, k_ref, v_ref, kv_ref, rates_ref, rates_other_ref, out_ref):
    weights = [w.astype(bf16) for w in head_init(init_ref)]
    all_gradients(c_ref[0], 0, weights, k_ref, v_ref, kv_ref, rates_ref, rates_other_ref, out_ref)


def second_kernel(
    c_ref, init_ref, grad_ref, k_ref, v_ref, kv_ref, rates_ref, rates_other_ref, out_ref, state_ref, wb_ref
):
    init = head_init(init_ref)
    state = updated(init, init, grad_ref)
    weights = [w.astype(bf16) for w in state]
    for i in range(3):
        state_ref[i] = state[i]
        wb_ref[i] = weights[i]
    all_gradients(c_ref[0], 1, weights, k_ref, v_ref, kv_ref, rates_ref, rates_other_ref, out_ref)


def apply_half(q, weights):
    gate = dot(q, weights[0], NT)
    up = dot(q, weights[1], NT)
    hidden = (gate * jax.nn.sigmoid(gate) * up).astype(bf16)
    return dot(hidden, weights[2], NN).astype(bf16).reshape(8, 1, 64, 256)


def apply_both(c, weights, q_ref, q_other_ref, out_ref):
    out_ref[:, pl.ds(c, 1)] = apply_half(q_ref[0], weights)
    out_ref[:, pl.ds(1 - c, 1)] = apply_half(q_other_ref[...], weights)


def apply_kernel(c_ref, wb_ref, q_ref, q_other_ref, out_ref):
    apply_both(c_ref[0], [wb_ref[0], wb_ref[1], wb_ref[2]], q_ref, q_other_ref, out_ref)


def last_kernel(c_ref, init_ref, state_ref, grad_ref, q_ref, q_other_ref, out_ref):
    state = updated([state_ref[i] for i in range(3)], head_init(init_ref), grad_ref)
    apply_both(c_ref[0], [w.astype(bf16) for w in state], q_ref, q_other_ref, out_ref)


def sum_kernel(part_ref, out_ref):
    total = jnp.sum(part_ref[...].astype(f32), axis=0, keepdims=True)
    out_ref[...] = jnp.broadcast_to(total.astype(bf16), out_ref.shape)


def whole(shape):
    return pl.BlockSpec(shape, lambda i, c: (0,) * len(shape))


def token_spec(block):
    return pl.BlockSpec((1, 512, 256), lambda i, c: (block, 0, c[0]))


INIT = pl.BlockSpec((3, 1, 256, 256), lambda i, c: (0, c[0], 0, 0))
GRAD = ((768, 256), bf16)
STATE = ((3, 256, 256), f32)
WEIGHTS = ((3, 256, 256), bf16)
RESULT = ((8, 2, 64, 256), bf16)


def call(kernel, in_specs, outs, name):
    many = len(outs) > 1
    specs = [whole(shape) for shape, _ in outs]
    shapes = [jax.ShapeDtypeStruct(shape, dtype) for shape, dtype in outs]
    return pl.pallas_call(
        kernel,
        grid_spec=pltpu.PrefetchScalarGridSpec(
            num_scalar_prefetch=1,
            grid=(1,),
            in_specs=in_specs,
            out_specs=specs if many else specs[0],
        ),
        out_shape=shapes if many else shapes[0],
        name=name,
    )


def exchange(array, axes):
    return lax.all_to_all(array, axes, split_axis=0, concat_axis=0, tiled=True)


def reduced(partial):
    parts = exchange(partial.reshape(32, 24, 256), ("x", "z"))
    total = pl.pallas_call(
        sum_kernel, out_shape=jax.ShapeDtypeStruct((32, 24, 256), bf16), name="sum_parts"
    )(parts)
    return exchange(total, ("x", "z")).reshape(768, 256)


def body(query_tokens, key_tokens, value_tokens, token_rates, fast_init):
    core = lax.axis_index("c")
    c = core.astype(jnp.int32).reshape(1)
    swap = [(0, 1), (1, 0)]

    def others(array):
        return jnp.where(core == 0, array[..., 256:], array[..., :256])

    kv_first = lax.ppermute(
        jnp.stack([others(key_tokens[0]), others(value_tokens[0])]), "c", swap
    )
    rates_other = lax.ppermute(
        jnp.where(core == 0, token_rates[:, :, 1], token_rates[:, :, 0]), "c", swap
    )
    rest = lax.ppermute(
        jnp.stack(
            [
                others(key_tokens[1]),
                others(value_tokens[1]),
                others(query_tokens[0]),
                others(query_tokens[1]),
            ]
        ),
        "c",
        swap,
    )
    grad_specs = [
        token_spec(0),
        token_spec(0),
        whole((2, 512, 256)),
        whole((3, 2, 2, 512)),
        whole((3, 2, 512)),
    ]
    grad_specs_second = [token_spec(1), token_spec(1)] + grad_specs[2:]
    first = call(first_kernel, [INIT] + grad_specs, [GRAD], "first_gradients")(
        c, fast_init, key_tokens, value_tokens, kv_first, token_rates, rates_other
    )
    summed = reduced(first)
    second, state, weights = call(
        second_kernel, [INIT, whole((768, 256))] + grad_specs_second, [GRAD, STATE, WEIGHTS], "second_gradients"
    )(c, fast_init, summed, key_tokens, value_tokens, rest[:2], token_rates, rates_other)
    out_first = call(
        apply_kernel, [whole((3, 256, 256)), token_spec(0), whole((512, 256))], [RESULT], "apply_first"
    )(c, weights, query_tokens, rest[2])
    summed = reduced(second)
    out_first = exchange(out_first.reshape(16, 64, 256), ("y", "c"))
    out_second = call(
        last_kernel,
        [INIT, whole((3, 256, 256)), whole((768, 256)), token_spec(1), whole((512, 256))],
        [RESULT],
        "apply_second",
    )(c, fast_init, state, summed, query_tokens, rest[3])
    out_second = exchange(out_second.reshape(16, 64, 256), ("y", "c"))
    return jnp.stack(
        [jnp.transpose(o, (1, 0, 2)).reshape(64, 4096) for o in (out_first, out_second)]
    )


def solution(mesh):
    fine = Mesh(mesh.devices.reshape(4, 8, 2, 8), ("x", "z", "c", "y"))
    seq = ("x", "z", "c")
    return jax.shard_map(
        body,
        mesh=fine,
        in_specs=(
            P(None, seq, "y"),
            P(None, seq, "y"),
            P(None, seq, "y"),
            P(None, None, "y", seq),
            P(None, "y", None, None),
        ),
        out_specs=P(None, (*seq, "y"), None),
        check_vma=False,
    )
```

```python
import jax
import jax.numpy as jnp
from jax import lax
from jax.experimental import pallas as pl
from jax.experimental.pallas import tpu as pltpu
from jax.sharding import Mesh, PartitionSpec as P


step_size = 0.05
eps_grad = 1e-05
eps_row = 1e-06
f32 = jnp.float32
bf16 = jnp.bfloat16
NT = (((1,), (1,)), ((), ()))
NN = (((1,), (0,)), ((), ()))
ROWS = 8


def dot(a, b, dims):
    return lax.dot_general(a, b, dims, preferred_element_type=f32)


def head_init(init_ref, kind):
    return [
        jnp.transpose(init_ref[0, 0].astype(f32)).astype(kind),
        jnp.transpose(init_ref[1, 0].astype(f32)).astype(kind),
        init_ref[2, 0].astype(kind),
    ]


def row_mean(w, i):
    return jnp.mean(w * w, axis=1 if i == 2 else 0, keepdims=True)


def gradients(keys, values, rate_gate, rate_up, rate_down, w_gate, w_up, w_down):
    gate = dot(w_gate, keys, NT)
    up = dot(w_up, keys, NT)
    err = dot(w_down, values, NT)
    sig = jax.nn.sigmoid(gate)
    silu = gate * sig
    hidden = (silu * up).astype(bf16)
    scaled = (hidden.astype(f32) * rate_down).astype(bf16)
    gate_grad = err * up * sig * (1.0 + gate * (1.0 - sig))
    gate_scaled = (gate_grad * rate_gate).astype(bf16)
    up_scaled = (err * silu * rate_up).astype(bf16)
    return (
        dot(gate_scaled, keys, NN),
        dot(up_scaled, keys, NN),
        dot(scaled, values, NN),
    )


def updated(state, init, grad_ref):
    result = []
    for i in range(3):
        grad = grad_ref[256 * i : 256 * (i + 1), :].astype(f32)
        rms = jnp.sqrt(jnp.mean(grad * grad, keepdims=True) + eps_grad)
        stepped = state[i] + grad * (step_size / rms)
        target = jnp.sqrt(row_mean(init[i], i))
        result.append(stepped * (target * lax.rsqrt(row_mean(stepped, i) + eps_row)))
    return result


def prepare_kernel(at, init_ref, out_ref):
    for i, w in enumerate(head_init(init_ref, f32)):
        out_ref[i] = w


def first_kernel(at, init_ref, k_ref, v_ref, rates_ref, out_ref):
    rates = [rates_ref[i, 0, pl.ds(at[0], 1), :] for i in (0, 1, 2)]
    grads = gradients(k_ref[0], v_ref[0], *rates, *head_init(init_ref, bf16))
    for i in range(3):
        out_ref[256 * i : 256 * (i + 1), :] = grads[i].astype(out_ref.dtype)


def second_kernel(at, init_ref, grad_ref, own_ref, other_ref, rates_ref, rates_other_ref, out_ref, state_ref, wb_ref):
    init = [init_ref[i] for i in range(3)]
    state = updated(init, init, grad_ref)
    weights = [w.astype(bf16) for w in state]
    for i in range(3):
        state_ref[i] = state[i]
        wb_ref[i] = weights[i]
    own = gradients(
        own_ref[0], own_ref[1], *[rates_ref[i, 1, pl.ds(at[0], 1), :] for i in (0, 1, 2)], *weights
    )
    other = gradients(
        other_ref[0], other_ref[1], *[rates_other_ref[i : i + 1, :] for i in (0, 1, 2)], *weights
    )
    for i in range(3):
        out_ref[256 * i : 256 * (i + 1), :] = (own[i] + other[i]).astype(bf16)


def applied(q, weights):
    gate = dot(q, weights[0], NT)
    up = dot(q, weights[1], NT)
    hidden = (gate * jax.nn.sigmoid(gate) * up).astype(bf16)
    return dot(hidden, weights[2], NN).astype(bf16)


def apply_first_kernel(at, own_ref, other_ref, q_ref, *refs):
    outs, scratch = refs[:-1], refs[-1]
    for weights_ref, head in ((own_ref, at[0]), (other_ref, 1 - at[0])):
        cols = pl.ds(pl.multiple_of(head * 256, 256), 256)
        weights = [weights_ref[i] for i in range(3)]
        scratch[:, :, cols] = applied(q_ref[0, :, cols], weights).reshape(ROWS, 64, 256)
    for d in range(ROWS):
        outs[d][...] = scratch[lax.rem(at[1] + d, ROWS)]


def gather_first_kernel(at, *refs):
    out_ref = refs[-1]
    for d in range(ROWS):
        source = lax.rem(at[1] + ROWS - d, ROWS)
        out_ref[0, :, pl.ds(pl.multiple_of(source * 512, 512), 512)] = refs[d][...]


def last_kernel(at, init_ref, state_ref, grad_ref, own_ref, other_ref, out_ref):
    state = updated([state_ref[i] for i in range(3)], [init_ref[i] for i in range(3)], grad_ref)
    weights = [w.astype(bf16) for w in state]
    for q, core in ((own_ref[2], at[0]), (other_ref[2], 1 - at[0])):
        out_ref[:, pl.ds(core, 1)] = applied(q, weights).reshape(ROWS, 1, 64, 256)


def gather_second_kernel(at, parts_ref, prev_ref, out_ref):
    for head in range(16):
        out_ref[0, :, 256 * head : 256 * (head + 1)] = parts_ref[head]


def whole(shape):
    return pl.BlockSpec(shape, lambda i, at: (0,) * len(shape))


VMEM = pl.BlockSpec(memory_space=pltpu.VMEM)
HEAD = pl.BlockSpec((3, 1, 256, 256), lambda i, at: (0, at[0], 0, 0))
TOKENS = pl.BlockSpec((1, 512, 256), lambda i, at: (0, 0, at[0]))
RATES = whole((3, 2, 2, 512))


def call(kernel, in_specs, outs, out_specs=None, scratch=(), aliases=None):
    specs = out_specs or [whole(shape) for shape, _ in outs]
    shapes = [jax.ShapeDtypeStruct(shape, dtype) for shape, dtype in outs]
    if len(outs) == 1:
        specs, shapes = specs[0], shapes[0]
    made = pl.pallas_call(
        kernel,
        grid_spec=pltpu.PrefetchScalarGridSpec(
            num_scalar_prefetch=1,
            grid=(1,),
            in_specs=in_specs,
            out_specs=specs,
            scratch_shapes=scratch,
        ),
        out_shape=shapes,
        input_output_aliases=aliases or {},
    )

    def run(at, *args):
        placed = [
            pltpu.with_memory_space_constraint(a, pltpu.VMEM) if s is VMEM else a
            for a, s in zip(args, in_specs)
        ]
        return made(at, *placed)

    return run


def exchange(array, axes):
    return lax.all_to_all(array, axes, split_axis=0, concat_axis=0, tiled=True)


def reduced(partial):
    parts = exchange(partial.reshape(32, 24, 256), ("x", "z"))
    total = jnp.sum(parts.astype(f32), axis=0, keepdims=True).astype(bf16)
    full = exchange(jnp.broadcast_to(total, (32, 24, 256)), ("x", "z"))
    return full.reshape(768, 256)


def swapped(array):
    return lax.ppermute(array, "c", [(0, 1), (1, 0)])


def program(query_tokens, key_tokens, value_tokens, token_rates, fast_init):
    core = lax.axis_index("c").astype(jnp.int32)
    row = lax.axis_index("y").astype(jnp.int32)
    at = jnp.stack([core, row])
    at_other = jnp.stack([1 - core, row])

    first_specs = [HEAD, TOKENS, TOKENS, RATES]
    first_args = (fast_init, key_tokens, value_tokens, token_rates)
    first_other = call(first_kernel, first_specs, [((768, 256), bf16)])(at_other, *first_args)
    first_got = swapped(first_other)
    first_own = call(first_kernel, first_specs, [((768, 256), f32)])(at, *first_args)
    first = (first_own + first_got.astype(f32)).astype(bf16)

    def half(which):
        return jnp.stack(
            [jnp.where(which == 0, a[1, :, :256], a[1, :, 256:]) for a in (key_tokens, value_tokens, query_tokens)]
        )

    other = swapped(half(1 - core))
    rates_other = swapped(jnp.where(core == 0, token_rates[:, 1, 1], token_rates[:, 1, 0]))
    own = half(core)
    init = call(prepare_kernel, [HEAD], [((3, 256, 256), f32)])(at, fast_init)

    summed = reduced(first)
    second, state, weights = call(
        second_kernel,
        [VMEM, VMEM, VMEM, VMEM, RATES, whole((3, 512))],
        [((768, 256), bf16), ((3, 256, 256), f32), ((3, 256, 256), bf16)],
    )(at, init, summed, own, other, token_rates, rates_other)

    weights_other = swapped(weights)
    pieces = call(
        apply_first_kernel,
        [whole((3, 256, 256)), whole((3, 256, 256)), pl.BlockSpec((1, 512, 512), lambda i, at: (0, 0, 0))],
        [((64, 512), bf16)] * ROWS,
        scratch=[pltpu.VMEM((ROWS, 64, 512), bf16)],
    )(at, weights, weights_other, query_tokens)
    got = [pieces[0]]
    for d in range(1, ROWS):
        got.append(lax.ppermute(pieces[d], "y", [(j, (j + d) % ROWS) for j in range(ROWS)]))

    summed = reduced(second)
    result = call(
        last_kernel, [VMEM, VMEM, VMEM, VMEM, VMEM], [((ROWS, 2, 64, 256), bf16)]
    )(at, init, state, summed, own, other)
    result = exchange(result.reshape(16, 64, 256), ("y", "c"))
    out = call(
        gather_first_kernel,
        [whole((64, 512))] * ROWS,
        [((2, 64, 4096), bf16)],
        [pl.BlockSpec((1, 64, 4096), lambda i, at: (0, 0, 0))],
    )(at, *got)
    return call(
        gather_second_kernel,
        [VMEM, pl.BlockSpec(memory_space=pl.ANY)],
        [((2, 64, 4096), bf16)],
        [pl.BlockSpec((1, 64, 4096), lambda i, at: (1, 0, 0))],
        aliases={2: 0},
    )(at, result, out)


def solution(mesh):
    fine = Mesh(mesh.devices.reshape(4, 8, 2, 8), ("x", "z", "c", "y"))
    seq = ("x", "z", "c")
    return jax.shard_map(
        program,
        mesh=fine,
        in_specs=(
            P(None, seq, "y"),
            P(None, seq, "y"),
            P(None, seq, "y"),
            P(None, None, "y", seq),
            P(None, "y", None, None),
        ),
        out_specs=P(None, (*seq, "y"), None),
        check_vma=False,
    )
```

```python
import jax
import jax.numpy as jnp
from jax import lax
from jax.experimental import pallas as pl
from jax.experimental.pallas import tpu as pltpu
from jax.sharding import Mesh, PartitionSpec as P


step_size = 0.05
eps_grad = 1e-05
eps_row = 1e-06
f32 = jnp.float32
bf16 = jnp.bfloat16
NT = (((1,), (1,)), ((), ()))
NN = (((1,), (0,)), ((), ()))
ROWS = 8


def dot(a, b, dims):
    return lax.dot_general(a, b, dims, preferred_element_type=f32)


def row_mean(w, i):
    return jnp.mean(w * w, axis=1 if i == 2 else 0, keepdims=True)


def gradients(keys, values, rate_gate, rate_up, rate_down, w_gate, w_up, w_down):
    gate = dot(w_gate, keys, NT)
    up = dot(w_up, keys, NT)
    err = dot(w_down, values, NT)
    sig = jax.nn.sigmoid(gate)
    silu = gate * sig
    hidden = (silu * up).astype(bf16)
    scaled = (hidden.astype(f32) * rate_down).astype(bf16)
    gate_grad = err * up * sig * (1.0 + gate * (1.0 - sig))
    gate_scaled = (gate_grad * rate_gate).astype(bf16)
    up_scaled = (err * silu * rate_up).astype(bf16)
    return (
        dot(gate_scaled, keys, NN),
        dot(up_scaled, keys, NN),
        dot(scaled, values, NN),
    )


def updated(state, init, grad_ref):
    result = []
    for i in range(3):
        grad = grad_ref[256 * i : 256 * (i + 1), :].astype(f32)
        rms = jnp.sqrt(jnp.mean(grad * grad, keepdims=True) + eps_grad)
        stepped = state[i] + grad * (step_size / rms)
        target = jnp.sqrt(row_mean(init[i], i))
        result.append(stepped * (target * lax.rsqrt(row_mean(stepped, i) + eps_row)))
    return result


def first_kernel(at, init_ref, k_ref, v_ref, rates_ref, other_ref, own_ref):
    for head, out_ref in ((1 - at[0], other_ref), (at[0], own_ref)):
        cols = pl.ds(pl.multiple_of(head * 256, 256), 256)
        rates = [rates_ref[i, 0, pl.ds(head, 1), :] for i in range(3)]
        weights = [
            jnp.transpose(init_ref[0, head]),
            jnp.transpose(init_ref[1, head]),
            init_ref[2, head],
        ]
        grads = gradients(k_ref[0, :, cols], v_ref[0, :, cols], *rates, *weights)
        for i in range(3):
            out_ref[256 * i : 256 * (i + 1), :] = grads[i].astype(out_ref.dtype)


def second_kernel(init_ref, grad_ref, own_ref, other_ref, rates_own_ref, rates_other_ref, out_ref, state_ref):
    init = [init_ref[i].astype(f32) for i in range(3)]
    state = updated(init, init, grad_ref)
    weights = [w.astype(bf16) for w in state]
    for i in range(3):
        state_ref[i] = state[i]
    own = gradients(own_ref[0], own_ref[1], *[rates_own_ref[i : i + 1, :] for i in range(3)], *weights)
    other = gradients(other_ref[0], other_ref[1], *[rates_other_ref[i : i + 1, :] for i in range(3)], *weights)
    for i in range(3):
        out_ref[256 * i : 256 * (i + 1), :] = (own[i] + other[i]).astype(bf16)


def applied(q, weights):
    gate = dot(q, weights[0], NT)
    up = dot(q, weights[1], NT)
    hidden = (gate * jax.nn.sigmoid(gate) * up).astype(bf16)
    return dot(hidden, weights[2], NN).astype(bf16).reshape(ROWS, 1, 1, 64, 256)


def apply_first_kernel(at, state_ref, own_ref, other_ref, out_ref):
    weights = [state_ref[i].astype(bf16) for i in range(3)]
    for q, core in ((own_ref[2], at[0]), (other_ref[2], 1 - at[0])):
        out_ref[:, pl.ds(core, 1)] = applied(q, weights)


def last_kernel(at, init_ref, state_ref, grad_ref, own_ref, other_ref, prev_ref, out_ref):
    state = updated([state_ref[i] for i in range(3)], [init_ref[i].astype(f32) for i in range(3)], grad_ref)
    weights = [w.astype(bf16) for w in state]
    for q, core in ((own_ref[3], at[0]), (other_ref[3], 1 - at[0])):
        out_ref[:, pl.ds(core, 1)] = applied(q, weights)


def assemble_kernel(parts_ref, out_ref):
    block, part = pl.program_id(0), pl.program_id(1)
    for head in range(16):
        out_ref[0, :, 256 * head : 256 * (head + 1)] = parts_ref[head, block, pl.ds(part * 32, 32)]


def whole(shape):
    return pl.BlockSpec(shape, lambda i, at: (0,) * len(shape))


def on_chip(array):
    return pltpu.with_memory_space_constraint(array, pltpu.VMEM)


def off_chip(array):
    return pltpu.with_memory_space_constraint(array, pltpu.HBM)


VMEM = pl.BlockSpec(memory_space=pltpu.VMEM)
LIMIT = pltpu.CompilerParams(vmem_limit_bytes=12 << 20)
ANY = pl.BlockSpec(memory_space=pl.ANY)


def call(kernel, in_specs, outs, out_specs=None, aliases=None):
    specs = out_specs or [whole(shape) for shape, _ in outs]
    shapes = [jax.ShapeDtypeStruct(shape, dtype) for shape, dtype in outs]
    if len(outs) == 1:
        specs, shapes = specs[0], shapes[0]
    return pl.pallas_call(
        kernel,
        grid_spec=pltpu.PrefetchScalarGridSpec(
            num_scalar_prefetch=1, grid=(1,), in_specs=in_specs, out_specs=specs
        ),
        out_shape=shapes,
        input_output_aliases=aliases or {},
        compiler_params=LIMIT,
    )


def exchange(array, axes):
    return lax.all_to_all(array, axes, split_axis=0, concat_axis=0, tiled=True)


def scattered(partial):
    parts = exchange(partial.reshape(32, 24, 256), ("x", "z"))
    return jnp.sum(parts.astype(f32), axis=0, keepdims=True)


def gathered(total):
    full = exchange(jnp.broadcast_to(total.astype(bf16), (32, 24, 256)), ("x", "z"))
    return on_chip(full.reshape(768, 256))


def swapped(array):
    return lax.ppermute(array, "c", [(0, 1), (1, 0)])


def program(query_tokens, key_tokens, value_tokens, token_rates, fast_init):
    core = lax.axis_index("c").astype(jnp.int32)
    at = core.reshape(1)

    first_other, first_own = call(
        first_kernel,
        [
            whole((3, 2, 256, 256)),
            pl.BlockSpec((1, 512, 512), lambda i, at: (0, 0, 0)),
            pl.BlockSpec((1, 512, 512), lambda i, at: (0, 0, 0)),
            whole((3, 2, 2, 512)),
        ],
        [((768, 256), bf16), ((768, 256), f32)],
    )(at, *[off_chip(a) for a in (fast_init, key_tokens, value_tokens, token_rates)])
    first_got = swapped(first_other)
    first = (first_own + first_got.astype(f32)).astype(bf16)
    first, query_tokens, key_tokens, value_tokens, token_rates, fast_init = lax.optimization_barrier(
        (first, query_tokens, key_tokens, value_tokens, token_rates, fast_init)
    )

    def pick(which, low, high):
        return jnp.where(which == 0, low, high)

    def half(which):
        return jnp.stack(
            [
                pick(which, a[..., :256], a[..., 256:])
                for a in (key_tokens[1], value_tokens[1], query_tokens[0], query_tokens[1])
            ]
        )

    other = swapped(half(1 - core))
    rates_other = swapped(pick(1 - core, token_rates[:, 1, 0], token_rates[:, 1, 1]))
    own = half(core)
    rates_own = pick(core, token_rates[:, 1, 0], token_rates[:, 1, 1])
    init = pick(core, fast_init[:, 0], fast_init[:, 1])
    init = jnp.stack([init[0].T, init[1].T, init[2]])

    total = scattered(first)
    total, other, rates_other, own, rates_own, init = lax.optimization_barrier(
        (total, other, rates_other, own, rates_own, init)
    )
    summed = gathered(total)
    second, state = pl.pallas_call(
        second_kernel,
        in_specs=[VMEM] * 6,
        out_specs=[VMEM] * 2,
        out_shape=[
            jax.ShapeDtypeStruct((768, 256), bf16),
            jax.ShapeDtypeStruct((3, 256, 256), f32),
        ],
        name="second",
        compiler_params=LIMIT,
    )(on_chip(init), summed, on_chip(own), on_chip(other), on_chip(rates_own), on_chip(rates_other))

    tokens = (4, 512, 256)
    pieces = ((ROWS, 2, 2, 64, 256), bf16)
    out = call(
        apply_first_kernel,
        [whole((3, 256, 256)), whole(tokens), whole(tokens)],
        [pieces],
        [pl.BlockSpec((ROWS, 2, 1, 64, 256), lambda i, at: (0, 0, 0, 0, 0))],
    )(at, state, own, other)

    total = scattered(second)
    total, out = lax.optimization_barrier((total, out))
    summed = gathered(total)
    out = call(
        last_kernel,
        [VMEM, VMEM, VMEM, VMEM, VMEM, ANY],
        [pieces],
        [pl.BlockSpec((ROWS, 2, 1, 64, 256), lambda i, at: (0, 0, 1, 0, 0))],
        aliases={6: 0},
    )(at, on_chip(init), on_chip(state), summed, on_chip(own), on_chip(other), out)
    parts = exchange(out.reshape(16, 2, 64, 256), ("y", "c"))
    return pl.pallas_call(
        assemble_kernel,
        grid=(2, 2),
        in_specs=[VMEM],
        out_specs=pl.BlockSpec((1, 32, 4096), lambda i, j: (i, j, 0)),
        out_shape=jax.ShapeDtypeStruct((2, 64, 4096), bf16),
        name="assemble",
        compiler_params=LIMIT,
    )(on_chip(parts))


def solution(mesh):
    fine = Mesh(mesh.devices.reshape(4, 8, 2, 8), ("x", "z", "c", "y"))
    seq = ("x", "z", "c")
    return jax.shard_map(
        program,
        mesh=fine,
        in_specs=(
            P(None, seq, "y"),
            P(None, seq, "y"),
            P(None, seq, "y"),
            P(None, None, "y", seq),
            P(None, "y", None, None),
        ),
        out_specs=P(None, (*seq, "y"), None),
        check_vma=False,
    )
```

```python
import jax
import jax.numpy as jnp
from jax import lax
from jax.experimental import pallas as pl
from jax.experimental.pallas import tpu as pltpu
from jax.sharding import Mesh, PartitionSpec as P


step_size = 0.05
eps_grad = 1e-05
eps_row = 1e-06
f32 = jnp.float32
bf16 = jnp.bfloat16
NT = (((1,), (1,)), ((), ()))
NN = (((1,), (0,)), ((), ()))
ROWS = 8


def dot(a, b, dims):
    return lax.dot_general(a, b, dims, preferred_element_type=f32)


def row_mean(w, i):
    return jnp.mean(w * w, axis=1 if i == 2 else 0, keepdims=True)


def gradients(keys, values, rate_gate, rate_up, rate_down, w_gate, w_up, w_down):
    gate = dot(w_gate, keys, NT)
    up = dot(w_up, keys, NT)
    err = dot(w_down, values, NT)
    sig = jax.nn.sigmoid(gate)
    silu = gate * sig
    hidden = (silu * up).astype(bf16)
    scaled = (hidden.astype(f32) * rate_down).astype(bf16)
    gate_grad = err * up * sig * (1.0 + gate * (1.0 - sig))
    gate_scaled = (gate_grad * rate_gate).astype(bf16)
    up_scaled = (err * silu * rate_up).astype(bf16)
    return (
        dot(gate_scaled, keys, NN),
        dot(up_scaled, keys, NN),
        dot(scaled, values, NN),
    )


def updated(state, init, grad_ref):
    result = []
    for i in range(3):
        grad = grad_ref[256 * i : 256 * (i + 1), :].astype(f32)
        rms = jnp.sqrt(jnp.mean(grad * grad, keepdims=True) + eps_grad)
        stepped = state[i] + grad * (step_size / rms)
        target = jnp.sqrt(row_mean(init[i], i))
        result.append(stepped * (target * lax.rsqrt(row_mean(stepped, i) + eps_row)))
    return result


def first_kernel(at, init_ref, k_ref, v_ref, rates_ref, other_ref, own_ref):
    for head, out_ref in ((1 - at[0], other_ref), (at[0], own_ref)):
        cols = pl.ds(pl.multiple_of(head * 256, 256), 256)
        rates = [rates_ref[i, 0, pl.ds(head, 1), :] for i in range(3)]
        weights = [
            jnp.transpose(init_ref[0, head]),
            jnp.transpose(init_ref[1, head]),
            init_ref[2, head],
        ]
        grads = gradients(k_ref[0, :, cols], v_ref[0, :, cols], *rates, *weights)
        for i in range(3):
            out_ref[256 * i : 256 * (i + 1), :] = grads[i].astype(out_ref.dtype)


def second_kernel(init_ref, grad_ref, own_ref, other_ref, rates_own_ref, rates_other_ref, out_ref, state_ref, weights_ref):
    init = [init_ref[i].astype(f32) for i in range(3)]
    state = updated(init, init, grad_ref)
    weights = [w.astype(bf16) for w in state]
    for i in range(3):
        state_ref[i] = state[i]
        weights_ref[i] = weights[i]
    own = gradients(own_ref[0], own_ref[1], *[rates_own_ref[i : i + 1, :] for i in range(3)], *weights)
    other = gradients(other_ref[0], other_ref[1], *[rates_other_ref[i : i + 1, :] for i in range(3)], *weights)
    for i in range(3):
        out_ref[256 * i : 256 * (i + 1), :] = (own[i] + other[i]).astype(bf16)


def applied(q, weights):
    gate = dot(q, weights[0], NT)
    up = dot(q, weights[1], NT)
    hidden = (gate * jax.nn.sigmoid(gate) * up).astype(bf16)
    return dot(hidden, weights[2], NN).astype(bf16)


def apply_first_kernel(at, own_ref, other_ref, q_ref, *refs):
    outs, scratch = refs[:-1], refs[-1]
    for weights_ref, head in ((own_ref, at[0]), (other_ref, 1 - at[0])):
        cols = pl.ds(pl.multiple_of(head * 256, 256), 256)
        weights = [weights_ref[i] for i in range(3)]
        scratch[:, :, cols] = applied(q_ref[:, cols], weights).reshape(ROWS, 64, 256)
    for d in range(ROWS):
        outs[d][...] = scratch[lax.rem(at[1] + d, ROWS)]


def last_kernel(at, init_ref, state_ref, grad_ref, own_ref, other_ref, out_ref):
    state = updated([state_ref[i] for i in range(3)], [init_ref[i].astype(f32) for i in range(3)], grad_ref)
    weights = [w.astype(bf16) for w in state]
    for q, core in ((own_ref[2], at[0]), (other_ref[2], 1 - at[0])):
        out_ref[:, pl.ds(core, 1)] = applied(q, weights).reshape(ROWS, 1, 64, 256)


def assemble_kernel(at, *refs):
    pieces, parts_ref, out_ref = refs[:ROWS], refs[ROWS], refs[ROWS + 1]
    rows = pl.ds(pl.program_id(1) * 32, 32)

    @pl.when(pl.program_id(0) == 0)
    def _():
        for d in range(ROWS):
            source = lax.rem(at[1] + ROWS - d, ROWS)
            out_ref[0, :, pl.ds(pl.multiple_of(source * 512, 512), 512)] = pieces[d][rows]

    @pl.when(pl.program_id(0) == 1)
    def _():
        for head in range(16):
            out_ref[0, :, 256 * head : 256 * (head + 1)] = parts_ref[head, rows]


def whole(shape):
    return pl.BlockSpec(shape, lambda i, at: (0,) * len(shape))


def on_chip(array):
    return pltpu.with_memory_space_constraint(array, pltpu.VMEM)


def off_chip(array):
    return pltpu.with_memory_space_constraint(array, pltpu.HBM)


VMEM = pl.BlockSpec(memory_space=pltpu.VMEM)
LIMIT = pltpu.CompilerParams(vmem_limit_bytes=12 << 20)
SCALARS = pl.BlockSpec(memory_space=pltpu.SMEM)


def call(kernel, in_specs, outs, out_specs=None, aliases=None):
    specs = out_specs or [whole(shape) for shape, _ in outs]
    shapes = [jax.ShapeDtypeStruct(shape, dtype) for shape, dtype in outs]
    if len(outs) == 1:
        specs, shapes = specs[0], shapes[0]
    return pl.pallas_call(
        kernel,
        grid_spec=pltpu.PrefetchScalarGridSpec(
            num_scalar_prefetch=1, grid=(1,), in_specs=in_specs, out_specs=specs
        ),
        out_shape=shapes,
        input_output_aliases=aliases or {},
        compiler_params=LIMIT,
    )


def exchange(array, axes):
    return lax.all_to_all(array, axes, split_axis=0, concat_axis=0, tiled=True)


def scattered(partial):
    parts = exchange(partial.reshape(32, 24, 256), ("x", "z"))
    return lax.optimization_barrier(jnp.sum(parts.astype(f32), axis=0, keepdims=True))


def gathered(total):
    full = exchange(jnp.broadcast_to(total.astype(bf16), (32, 24, 256)), ("x", "z"))
    return on_chip(full.reshape(768, 256))


def swapped(array):
    return lax.ppermute(array, "c", [(0, 1), (1, 0)])


def program(query_tokens, key_tokens, value_tokens, token_rates, fast_init):
    core = lax.axis_index("c").astype(jnp.int32)
    at = jnp.stack([core, lax.axis_index("y").astype(jnp.int32)])

    first_other, first_own = call(
        first_kernel,
        [
            whole((3, 2, 256, 256)),
            pl.BlockSpec((1, 512, 512), lambda i, at: (0, 0, 0)),
            pl.BlockSpec((1, 512, 512), lambda i, at: (0, 0, 0)),
            whole((3, 2, 2, 512)),
        ],
        [((768, 256), bf16), ((768, 256), f32)],
    )(at, *[off_chip(a) for a in (fast_init, key_tokens, value_tokens, token_rates)])
    first_got = swapped(first_other)
    first = (first_own + first_got.astype(f32)).astype(bf16)
    first, query_tokens, key_tokens, value_tokens, token_rates, fast_init = lax.optimization_barrier(
        (first, query_tokens, key_tokens, value_tokens, token_rates, fast_init)
    )

    def pick(which, low, high):
        return jnp.where(which == 0, low, high)

    def half(which):
        return jnp.stack(
            [
                pick(which, a[..., :256], a[..., 256:])
                for a in (key_tokens[1], value_tokens[1], query_tokens[1])
            ]
        )

    other = swapped(half(1 - core))
    rates_other = swapped(pick(1 - core, token_rates[:, 1, 0], token_rates[:, 1, 1]))
    own = half(core)
    rates_own = pick(core, token_rates[:, 1, 0], token_rates[:, 1, 1])
    init = pick(core, fast_init[:, 0], fast_init[:, 1])
    init = jnp.stack([init[0].T, init[1].T, init[2]])

    total = scattered(first)
    queries = query_tokens[0]
    total, other, rates_other, own, rates_own, init, queries = lax.optimization_barrier(
        (total, other, rates_other, own, rates_own, init, queries)
    )
    summed = gathered(total)
    second, state, weights = pl.pallas_call(
        second_kernel,
        in_specs=[VMEM] * 6,
        out_specs=[VMEM] * 3,
        out_shape=[
            jax.ShapeDtypeStruct((768, 256), bf16),
            jax.ShapeDtypeStruct((3, 256, 256), f32),
            jax.ShapeDtypeStruct((3, 256, 256), bf16),
        ],
        name="second",
        compiler_params=LIMIT,
    )(on_chip(init), summed, on_chip(own), on_chip(other), on_chip(rates_own), on_chip(rates_other))

    weights_other = swapped(weights)
    pieces = pl.pallas_call(
        apply_first_kernel,
        in_specs=[SCALARS, VMEM, VMEM, VMEM],
        out_specs=[VMEM] * ROWS,
        out_shape=[jax.ShapeDtypeStruct((64, 512), bf16)] * ROWS,
        scratch_shapes=[pltpu.VMEM((ROWS, 64, 512), bf16)],
        name="apply_first",
        compiler_params=LIMIT,
    )(at, on_chip(weights), on_chip(weights_other), on_chip(queries))
    got = [pieces[0]]
    for d in range(1, ROWS):
        got.append(lax.ppermute(pieces[d], "y", [(j, (j + d) % ROWS) for j in range(ROWS)]))

    total = scattered(second)
    summed = gathered(total)
    result = call(
        last_kernel, [VMEM, VMEM, VMEM, VMEM, VMEM], [((ROWS, 2, 64, 256), bf16)]
    )(at, on_chip(init), on_chip(state), summed, on_chip(own), on_chip(other))
    parts = exchange(result.reshape(16, 64, 256), ("y", "c"))
    return pl.pallas_call(
        assemble_kernel,
        grid=(2, 2),
        in_specs=[SCALARS] + [VMEM] * (ROWS + 1),
        out_specs=pl.BlockSpec((1, 32, 4096), lambda i, j: (i, j, 0)),
        out_shape=jax.ShapeDtypeStruct((2, 64, 4096), bf16),
        name="assemble",
        compiler_params=LIMIT,
    )(at, *[on_chip(a) for a in got], on_chip(parts))


def solution(mesh):
    fine = Mesh(mesh.devices.reshape(4, 8, 2, 8), ("x", "z", "c", "y"))
    seq = ("x", "z", "c")
    return jax.shard_map(
        program,
        mesh=fine,
        in_specs=(
            P(None, seq, "y"),
            P(None, seq, "y"),
            P(None, seq, "y"),
            P(None, None, "y", seq),
            P(None, "y", None, None),
        ),
        out_specs=P(None, (*seq, "y"), None),
        check_vma=False,
    )
```

```python
import jax
import jax.numpy as jnp
from jax import lax
from jax.experimental import pallas as pl
from jax.experimental.pallas import tpu as pltpu
from jax.sharding import Mesh, PartitionSpec as P


step_size = 0.05
eps_grad = 1e-05
eps_row = 1e-06
f32 = jnp.float32
bf16 = jnp.bfloat16
NT = (((1,), (1,)), ((), ()))
NN = (((1,), (0,)), ((), ()))
ROWS = 8


def dot(a, b, dims):
    return lax.dot_general(a, b, dims, preferred_element_type=f32)


def row_mean(w, i):
    return jnp.mean(w * w, axis=1 if i == 2 else 0, keepdims=True)


def gradients(keys, values, rate_gate, rate_up, rate_down, w_gate, w_up, w_down):
    gate = dot(w_gate, keys, NT)
    up = dot(w_up, keys, NT)
    err = dot(w_down, values, NT)
    sig = jax.nn.sigmoid(gate)
    silu = gate * sig
    hidden = (silu * up).astype(bf16)
    scaled = (hidden.astype(f32) * rate_down).astype(bf16)
    gate_grad = err * up * sig * (1.0 + gate * (1.0 - sig))
    gate_scaled = (gate_grad * rate_gate).astype(bf16)
    up_scaled = (err * silu * rate_up).astype(bf16)
    return (
        dot(gate_scaled, keys, NN),
        dot(up_scaled, keys, NN),
        dot(scaled, values, NN),
    )


def updated(state, init, grad_ref):
    result = []
    for i in range(3):
        grad = grad_ref[256 * i : 256 * (i + 1), :].astype(f32)
        rms = jnp.sqrt(jnp.mean(grad * grad, keepdims=True) + eps_grad)
        stepped = state[i] + grad * (step_size / rms)
        target = jnp.sqrt(row_mean(init[i], i))
        result.append(stepped * (target * lax.rsqrt(row_mean(stepped, i) + eps_row)))
    return result


def first_kernel(at, init_ref, k_ref, v_ref, rates_ref, other_ref, own_ref):
    for head, out_ref in ((1 - at[0], other_ref), (at[0], own_ref)):
        cols = pl.ds(pl.multiple_of(head * 256, 256), 256)
        rates = [rates_ref[i, 0, pl.ds(head, 1), :] for i in range(3)]
        weights = [
            jnp.transpose(init_ref[0, head]),
            jnp.transpose(init_ref[1, head]),
            init_ref[2, head],
        ]
        grads = gradients(k_ref[0, :, cols], v_ref[0, :, cols], *rates, *weights)
        for i in range(3):
            out_ref[256 * i : 256 * (i + 1), :] = grads[i].astype(out_ref.dtype)


def second_kernel(init_ref, grad_ref, own_ref, other_ref, rates_own_ref, rates_other_ref, out_ref, state_ref, weights_ref):
    init = [init_ref[i].astype(f32) for i in range(3)]
    state = updated(init, init, grad_ref)
    weights = [w.astype(bf16) for w in state]
    for i in range(3):
        state_ref[i] = state[i]
        weights_ref[i] = weights[i]
    own = gradients(own_ref[0], own_ref[1], *[rates_own_ref[i : i + 1, :] for i in range(3)], *weights)
    other = gradients(other_ref[0], other_ref[1], *[rates_other_ref[i : i + 1, :] for i in range(3)], *weights)
    for i in range(3):
        out_ref[256 * i : 256 * (i + 1), :] = (own[i] + other[i]).astype(bf16)


def applied(q, weights):
    gate = dot(q, weights[0], NT)
    up = dot(q, weights[1], NT)
    hidden = (gate * jax.nn.sigmoid(gate) * up).astype(bf16)
    return dot(hidden, weights[2], NN).astype(bf16)


FIRST_LEVEL = ((2, 3, 4), (-3, -2), (1,), (-1,), (0,))


def apply_first_kernel(core_ref, row_ref, own_ref, other_ref, q_ref, *refs):
    outs, scratch = refs[:-1], refs[-1]
    for weights_ref, head in ((own_ref, core_ref[0]), (other_ref, 1 - core_ref[0])):
        cols = pl.ds(pl.multiple_of(head * 256, 256), 256)
        weights = [weights_ref[i] for i in range(3)]
        scratch[:, :, cols] = applied(q_ref[:, cols], weights).reshape(ROWS, 64, 256)
    for ahead, out_ref in zip(FIRST_LEVEL, outs):
        for i, d in enumerate(ahead):
            out_ref[i] = scratch[lax.rem(row_ref[0] + ROWS + d, ROWS)]


def last_kernel(at, init_ref, state_ref, grad_ref, own_ref, other_ref, out_ref):
    state = updated([state_ref[i] for i in range(3)], [init_ref[i].astype(f32) for i in range(3)], grad_ref)
    weights = [w.astype(bf16) for w in state]
    for q, core in ((own_ref[2], at[0]), (other_ref[2], 1 - at[0])):
        out_ref[:, pl.ds(core, 1)] = applied(q, weights).reshape(ROWS, 1, 64, 256)


def assemble_first_kernel(row_ref, here_ref, far_ahead_ref, far_behind_ref, ahead_ref, behind_ref, out_ref):
    for source, piece in (
        (0, here_ref[0]),
        (-3, far_ahead_ref[1]),
        (2, far_behind_ref[1]),
        (-1, ahead_ref[0]),
        (-4, ahead_ref[1]),
        (1, behind_ref[0]),
        (-2, behind_ref[1]),
        (3, behind_ref[2]),
    ):
        cols = lax.rem(row_ref[0] + ROWS + source, ROWS) * 512
        out_ref[0, :, pl.ds(pl.multiple_of(cols, 512), 512)] = piece


def assemble_second_kernel(parts_ref, prev_ref, out_ref):
    rows = pl.ds(pl.program_id(0) * 32, 32)
    for head in range(16):
        out_ref[0, :, 256 * head : 256 * (head + 1)] = parts_ref[head, rows]


def whole(shape):
    return pl.BlockSpec(shape, lambda i, at: (0,) * len(shape))


def on_chip(array):
    return pltpu.with_memory_space_constraint(array, pltpu.VMEM)


def off_chip(array):
    return pltpu.with_memory_space_constraint(array, pltpu.HBM)


VMEM = pl.BlockSpec(memory_space=pltpu.VMEM)
LIMIT = pltpu.CompilerParams(vmem_limit_bytes=12 << 20)
ANY = pl.BlockSpec(memory_space=pl.ANY)
SCALARS = pl.BlockSpec(memory_space=pltpu.SMEM)


def call(kernel, in_specs, outs, out_specs=None, aliases=None):
    specs = out_specs or [whole(shape) for shape, _ in outs]
    shapes = [jax.ShapeDtypeStruct(shape, dtype) for shape, dtype in outs]
    if len(outs) == 1:
        specs, shapes = specs[0], shapes[0]
    return pl.pallas_call(
        kernel,
        grid_spec=pltpu.PrefetchScalarGridSpec(
            num_scalar_prefetch=1, grid=(1,), in_specs=in_specs, out_specs=specs
        ),
        out_shape=shapes,
        input_output_aliases=aliases or {},
        compiler_params=LIMIT,
    )


def exchange(array, axes):
    return lax.all_to_all(array, axes, split_axis=0, concat_axis=0, tiled=True)


def scattered(partial):
    parts = exchange(partial.reshape(32, 24, 256), ("x", "z"))
    return lax.optimization_barrier(jnp.sum(parts.astype(f32), axis=0, keepdims=True))


def gathered(total):
    full = exchange(jnp.broadcast_to(total.astype(bf16), (32, 24, 256)), ("x", "z"))
    return on_chip(full.reshape(768, 256))


def swapped(array):
    return lax.ppermute(array, "c", [(0, 1), (1, 0)])


def program(query_tokens, key_tokens, value_tokens, token_rates, fast_init):
    core = lax.axis_index("c").astype(jnp.int32)
    at = core.reshape(1)
    row = lax.axis_index("y").astype(jnp.int32).reshape(1)

    first_other, first_own = call(
        first_kernel,
        [
            whole((3, 2, 256, 256)),
            pl.BlockSpec((1, 512, 512), lambda i, at: (0, 0, 0)),
            pl.BlockSpec((1, 512, 512), lambda i, at: (0, 0, 0)),
            whole((3, 2, 2, 512)),
        ],
        [((768, 256), bf16), ((768, 256), f32)],
    )(at, *[off_chip(a) for a in (fast_init, key_tokens, value_tokens, token_rates)])
    first_got = swapped(first_other)
    first = (first_own + first_got.astype(f32)).astype(bf16)
    first, query_tokens, key_tokens, value_tokens, token_rates, fast_init = lax.optimization_barrier(
        (first, query_tokens, key_tokens, value_tokens, token_rates, fast_init)
    )

    def pick(which, low, high):
        return jnp.where(which == 0, low, high)

    def half(which):
        return jnp.stack(
            [
                pick(which, a[..., :256], a[..., 256:])
                for a in (key_tokens[1], value_tokens[1], query_tokens[1])
            ]
        )

    other = swapped(half(1 - core))
    rates_other = swapped(pick(1 - core, token_rates[:, 1, 0], token_rates[:, 1, 1]))
    own = half(core)
    rates_own = pick(core, token_rates[:, 1, 0], token_rates[:, 1, 1])
    init = pick(core, fast_init[:, 0], fast_init[:, 1])
    init = jnp.stack([init[0].T, init[1].T, init[2]])

    total = scattered(first)
    queries = query_tokens[0]
    total, other, rates_other, own, rates_own, init, queries = lax.optimization_barrier(
        (total, other, rates_other, own, rates_own, init, queries)
    )
    summed = gathered(total)
    second, state, weights = pl.pallas_call(
        second_kernel,
        in_specs=[VMEM] * 6,
        out_specs=[VMEM] * 3,
        out_shape=[
            pltpu.HBM((768, 256), bf16),
            jax.ShapeDtypeStruct((3, 256, 256), f32),
            pltpu.HBM((3, 256, 256), bf16),
        ],
        name="second",
        compiler_params=LIMIT,
    )(on_chip(init), summed, on_chip(own), on_chip(other), on_chip(rates_own), on_chip(rates_other))

    weights_other = swapped(weights)
    far_ahead, far_behind, ahead, behind, here = pl.pallas_call(
        apply_first_kernel,
        in_specs=[SCALARS, SCALARS, VMEM, VMEM, VMEM],
        out_specs=[VMEM] * len(FIRST_LEVEL),
        out_shape=[(pltpu.HBM if len(d) < 3 else jax.ShapeDtypeStruct)((len(d), 64, 512), bf16) for d in FIRST_LEVEL],
        scratch_shapes=[pltpu.VMEM((ROWS, 64, 512), bf16)],
        name="apply_first",
        compiler_params=LIMIT,
    )(at, row, off_chip(weights), on_chip(weights_other), on_chip(queries))

    def sent(array, step):
        return lax.ppermute(array, "y", [(j, (j + step) % ROWS) for j in range(ROWS)])

    far_ahead = sent(far_ahead, 3)
    far_behind = sent(far_behind, -2)
    ahead = sent(jnp.concatenate([ahead, far_ahead[2:]]), 1)
    behind = sent(jnp.concatenate([behind, far_ahead[:1], far_behind[:1]]), -1)

    total = scattered(second)
    summed = gathered(total)
    result = call(
        last_kernel, [VMEM, VMEM, VMEM, VMEM, VMEM], [((ROWS, 2, 64, 256), bf16)]
    )(at, on_chip(init), on_chip(state), summed, on_chip(own), on_chip(other))
    parts = exchange(result.reshape(16, 64, 256), ("y", "c"))
    out = pl.pallas_call(
        assemble_first_kernel,
        grid=(1,),
        in_specs=[SCALARS] + [VMEM] * 5,
        out_specs=pl.BlockSpec((1, 64, 4096), lambda i: (0, 0, 0)),
        out_shape=jax.ShapeDtypeStruct((2, 64, 4096), bf16),
        name="assemble_first",
        compiler_params=LIMIT,
    )(row, off_chip(here), *[on_chip(a) for a in (far_ahead, far_behind, ahead, behind)])
    return pl.pallas_call(
        assemble_second_kernel,
        grid=(2,),
        in_specs=[VMEM, ANY],
        out_specs=pl.BlockSpec((1, 32, 4096), lambda i: (1, i, 0)),
        out_shape=jax.ShapeDtypeStruct((2, 64, 4096), bf16),
        input_output_aliases={1: 0},
        name="assemble_second",
        compiler_params=LIMIT,
    )(on_chip(parts), out)


def solution(mesh):
    fine = Mesh(mesh.devices.reshape(4, 8, 2, 8), ("x", "z", "c", "y"))
    seq = ("x", "z", "c")
    return jax.shard_map(
        program,
        mesh=fine,
        in_specs=(
            P(None, seq, "y"),
            P(None, seq, "y"),
            P(None, seq, "y"),
            P(None, None, "y", seq),
            P(None, "y", None, None),
        ),
        out_specs=P(None, (*seq, "y"), None),
        check_vma=False,
    )
```

```python
import jax
import jax.numpy as jnp
from jax import lax
from jax.experimental import pallas as pl
from jax.experimental.pallas import tpu as pltpu
from jax.sharding import Mesh, PartitionSpec as P


step_size = 0.05
eps_grad = 1e-05
eps_row = 1e-06
f32 = jnp.float32
bf16 = jnp.bfloat16
NT = (((1,), (1,)), ((), ()))
NN = (((1,), (0,)), ((), ()))
ROWS = 8


def dot(a, b, dims):
    return lax.dot_general(a, b, dims, preferred_element_type=f32)


def row_mean(w, i):
    return jnp.mean(w * w, axis=1 if i == 2 else 0, keepdims=True)


def gradients(keys, values, rate_gate, rate_up, rate_down, w_gate, w_up, w_down):
    gate = dot(w_gate, keys, NT)
    up = dot(w_up, keys, NT)
    err = dot(w_down, values, NT)
    sig = jax.nn.sigmoid(gate)
    silu = gate * sig
    hidden = (silu * up).astype(bf16)
    scaled = (hidden.astype(f32) * rate_down).astype(bf16)
    gate_grad = err * up * sig * (1.0 + gate * (1.0 - sig))
    gate_scaled = (gate_grad * rate_gate).astype(bf16)
    up_scaled = (err * silu * rate_up).astype(bf16)
    return (
        dot(gate_scaled, keys, NN),
        dot(up_scaled, keys, NN),
        dot(scaled, values, NN),
    )


def updated(state, targets, grad_ref):
    result = []
    for i in range(3):
        grad = grad_ref[256 * i : 256 * (i + 1), :].astype(f32)
        rms = jnp.sqrt(jnp.mean(grad * grad, keepdims=True) + eps_grad)
        stepped = state[i] + grad * (step_size / rms)
        result.append(stepped * (targets[i] * lax.rsqrt(row_mean(stepped, i) + eps_row)))
    return result


def first_kernel(at, init_ref, k_ref, v_ref, rates_ref, other_ref, own_ref):
    for head, out_ref in ((1 - at[0], other_ref), (at[0], own_ref)):
        cols = pl.ds(pl.multiple_of(head * 256, 256), 256)
        rates = [rates_ref[i, 0, pl.ds(head, 1), :] for i in range(3)]
        weights = [
            jnp.transpose(init_ref[0, head]),
            jnp.transpose(init_ref[1, head]),
            init_ref[2, head],
        ]
        grads = gradients(k_ref[0, :, cols], v_ref[0, :, cols], *rates, *weights)
        for i in range(3):
            out_ref[256 * i : 256 * (i + 1), :] = grads[i].astype(out_ref.dtype)


KEPT = (1032, 256)


def second_kernel(init_ref, grad_ref, own_ref, other_ref, rates_own_ref, rates_other_ref, out_ref, kept_ref):
    init = [init_ref[i].astype(f32) for i in range(3)]
    targets = [jnp.sqrt(row_mean(w, i)) for i, w in enumerate(init)]
    state = updated(init, targets, grad_ref)
    weights = [w.astype(bf16) for w in state]
    for i in range(3):
        kept_ref[256 * i : 256 * (i + 1), :] = state[i]
    kept_ref[768:1024, :] = jnp.broadcast_to(targets[2], (256, 256))
    kept_ref[1024:1025, :] = targets[0]
    kept_ref[1025:1026, :] = targets[1]
    kept_ref[1026:1032, :] = jnp.zeros((6, 256), f32)
    own = gradients(own_ref[0], own_ref[1], *[rates_own_ref[i : i + 1, :] for i in range(3)], *weights)
    other = gradients(other_ref[0], other_ref[1], *[rates_other_ref[i : i + 1, :] for i in range(3)], *weights)
    for i in range(3):
        out_ref[256 * i : 256 * (i + 1), :] = (own[i] + other[i]).astype(bf16)


def state_of(kept_ref):
    return [kept_ref[256 * i : 256 * (i + 1), :] for i in range(3)]


def applied(q, weights):
    gate = dot(q, weights[0], NT)
    up = dot(q, weights[1], NT)
    hidden = (gate * jax.nn.sigmoid(gate) * up).astype(bf16)
    return dot(hidden, weights[2], NN).astype(bf16)


def prepare_kernel(core_ref, k_ref, v_ref, q_ref, init_ref, rates_ref, own_ref, other_ref, w_ref, rates_own_ref, rates_other_ref):
    for head, out_ref, rates_out_ref in (
        (core_ref[0], own_ref, rates_own_ref),
        (1 - core_ref[0], other_ref, rates_other_ref),
    ):
        cols = pl.ds(pl.multiple_of(head * 256, 256), 256)
        out_ref[0] = k_ref[0, :, cols]
        out_ref[1] = v_ref[0, :, cols]
        out_ref[2] = q_ref[1, :, cols]
        out_ref[3] = q_ref[0, :, cols]
        for i in range(3):
            rates_out_ref[i : i + 1, :] = rates_ref[i, 1, pl.ds(head, 1), :]
    for i in range(3):
        w = init_ref[i, core_ref[0]]
        w_ref[i] = w if i == 2 else jnp.transpose(w)


FIRST_LEVEL = ((2, 3, 4), (-3, -2), (1,), (-1,), (0,))
SOURCES = (0, -3, 2, -1, -4, 1, -2, 3)


def apply_first_kernel(row_ref, kept_ref, own_ref, other_ref, *refs):
    outs, scratch = refs[:-1], refs[-1]
    weights = [w.astype(bf16) for w in state_of(kept_ref)]
    for q, side in ((own_ref[3], 0), (other_ref[3], 1)):
        scratch[:, side] = applied(q, weights).reshape(ROWS, 64, 256)
    for ahead, out_ref in zip(FIRST_LEVEL, outs):
        for i, d in enumerate(ahead):
            out_ref[i] = scratch[lax.rem(row_ref[0] + ROWS + d, ROWS)]


def last_kernel(at, kept_ref, grad_ref, own_ref, other_ref, out_ref):
    targets = [kept_ref[1024:1025, :], kept_ref[1025:1026, :], kept_ref[768:1024, :]]
    state = updated(state_of(kept_ref), targets, grad_ref)
    weights = [w.astype(bf16) for w in state]
    for q, core in ((own_ref[2], at[0]), (other_ref[2], 1 - at[0])):
        out_ref[:, pl.ds(core, 1)] = applied(q, weights).reshape(ROWS, 1, 64, 256)


def total_kernel(parts_ref, out_ref):
    total = jnp.sum(parts_ref[...].astype(f32), axis=0, keepdims=True)
    out_ref[...] = jnp.broadcast_to(total.astype(bf16), out_ref.shape)


def pieces_of(here_ref, far_ahead_ref, far_behind_ref, ahead_ref, behind_ref, side):
    return (
        here_ref[0, side],
        far_ahead_ref[1, side],
        far_behind_ref[1, side],
        ahead_ref[0, side],
        ahead_ref[1, side],
        behind_ref[0, side],
        behind_ref[1, side],
        behind_ref[2, side],
    )


def collect_kernel(*refs):
    for i, piece in enumerate(pieces_of(*refs[:5], 1)):
        refs[5][i] = piece


def assemble_first_kernel(core_ref, row_ref, *refs):
    swapped_ref, out_ref = refs[5], refs[6]
    for i, (source, piece) in enumerate(zip(SOURCES, pieces_of(*refs[:5], 0))):
        first = lax.rem(row_ref[0] + ROWS + source, ROWS) * 512
        own = pl.multiple_of(first + core_ref[0] * 256, 256)
        other = pl.multiple_of(first + (1 - core_ref[0]) * 256, 256)
        out_ref[0, :, pl.ds(own, 256)] = piece
        out_ref[0, :, pl.ds(other, 256)] = swapped_ref[i]


def assemble_second_kernel(parts_ref, prev_ref, out_ref):
    rows = pl.ds(pl.program_id(0) * 32, 32)
    for head in range(16):
        out_ref[0, :, 256 * head : 256 * (head + 1)] = parts_ref[head, rows]


def whole(shape):
    return pl.BlockSpec(shape, lambda i, at: (0,) * len(shape))


def on_chip(array):
    return pltpu.with_memory_space_constraint(array, pltpu.VMEM)


def off_chip(array):
    return pltpu.with_memory_space_constraint(array, pltpu.HBM)


VMEM = pl.BlockSpec(memory_space=pltpu.VMEM)
LIMIT = pltpu.CompilerParams(vmem_limit_bytes=12 << 20)
ANY = pl.BlockSpec(memory_space=pl.ANY)
SCALARS = pl.BlockSpec(memory_space=pltpu.SMEM)


def call(kernel, in_specs, outs, out_specs=None, aliases=None):
    specs = out_specs or [whole(shape) for shape, _ in outs]
    shapes = [jax.ShapeDtypeStruct(shape, dtype) for shape, dtype in outs]
    if len(outs) == 1:
        specs, shapes = specs[0], shapes[0]
    return pl.pallas_call(
        kernel,
        grid_spec=pltpu.PrefetchScalarGridSpec(
            num_scalar_prefetch=1, grid=(1,), in_specs=in_specs, out_specs=specs
        ),
        out_shape=shapes,
        input_output_aliases=aliases or {},
        compiler_params=LIMIT,
    )


def exchange(array, axes):
    return lax.all_to_all(array, axes, split_axis=0, concat_axis=0, tiled=True)


def scattered(partial):
    parts = exchange(partial.reshape(32, 24, 256), ("x", "z"))
    return pl.pallas_call(
        total_kernel,
        in_specs=[VMEM],
        out_specs=VMEM,
        out_shape=jax.ShapeDtypeStruct((32, 24, 256), bf16),
        name="total",
        compiler_params=LIMIT,
    )(on_chip(parts))


def gathered(total):
    full = exchange(total, ("x", "z"))
    return on_chip(full.reshape(768, 256))


def swapped(array):
    return lax.ppermute(array, "c", [(0, 1), (1, 0)])


def program(query_tokens, key_tokens, value_tokens, token_rates, fast_init):
    core = lax.axis_index("c").astype(jnp.int32)
    at = core.reshape(1)
    row = lax.axis_index("y").astype(jnp.int32).reshape(1)

    first_other, first_own = call(
        first_kernel,
        [
            whole((3, 2, 256, 256)),
            pl.BlockSpec((1, 512, 512), lambda i, at: (0, 0, 0)),
            pl.BlockSpec((1, 512, 512), lambda i, at: (0, 0, 0)),
            whole((3, 2, 2, 512)),
        ],
        [((768, 256), bf16), ((768, 256), f32)],
    )(at, *[off_chip(a) for a in (fast_init, key_tokens, value_tokens, token_rates)])
    first_got = swapped(first_other)
    first = (first_own + first_got.astype(f32)).astype(bf16)
    first, query_tokens, key_tokens, value_tokens, token_rates, fast_init = lax.optimization_barrier(
        (first, query_tokens, key_tokens, value_tokens, token_rates, fast_init)
    )

    tokens = (4, 512, 256)
    own, other, init, rates_own, rates_other = call(
        prepare_kernel,
        [
            pl.BlockSpec((1, 512, 512), lambda i, at: (1, 0, 0)),
            pl.BlockSpec((1, 512, 512), lambda i, at: (1, 0, 0)),
            whole((2, 512, 512)),
            whole((3, 2, 256, 256)),
            whole((3, 2, 2, 512)),
        ],
        [(tokens, bf16), (tokens, bf16), ((3, 256, 256), bf16), ((3, 512), f32), ((3, 512), f32)],
    )(at, *[off_chip(a) for a in (key_tokens, value_tokens, query_tokens, fast_init, token_rates)])
    other = swapped(other)
    rates_other = swapped(rates_other)

    total = scattered(first)
    total, other, rates_other, own, rates_own, init = lax.optimization_barrier(
        (total, other, rates_other, own, rates_own, init)
    )
    summed = gathered(total)
    second, kept = pl.pallas_call(
        second_kernel,
        in_specs=[VMEM] * 6,
        out_specs=[VMEM] * 2,
        out_shape=[
            pltpu.HBM((768, 256), bf16),
            jax.ShapeDtypeStruct(KEPT, f32),
        ],
        name="second",
        compiler_params=LIMIT,
    )(on_chip(init), summed, on_chip(own), on_chip(other), rates_own, rates_other)

    far_ahead, far_behind, ahead, behind, here = pl.pallas_call(
        apply_first_kernel,
        in_specs=[SCALARS, VMEM, VMEM, VMEM],
        out_specs=[VMEM] * len(FIRST_LEVEL),
        out_shape=[
            (pltpu.HBM if d in ((1,), (-1,)) else jax.ShapeDtypeStruct)((len(d), 2, 64, 256), bf16)
            for d in FIRST_LEVEL
        ],
        scratch_shapes=[pltpu.VMEM((ROWS, 2, 64, 256), bf16)],
        name="apply_first",
        compiler_params=LIMIT,
    )(row, on_chip(kept), on_chip(own), on_chip(other))

    def sent(array, step):
        return lax.ppermute(array, "y", [(j, (j + step) % ROWS) for j in range(ROWS)])

    far_ahead = sent(far_ahead, 3)
    far_behind = sent(far_behind, -2)
    ahead = sent(jnp.concatenate([ahead, far_ahead[2:]]), 1)
    behind = sent(jnp.concatenate([behind, far_ahead[:1], far_behind[:1]]), -1)

    total = scattered(second)
    summed = gathered(total)
    result = call(
        last_kernel, [VMEM, VMEM, VMEM, VMEM], [((ROWS, 2, 64, 256), bf16)]
    )(at, on_chip(kept), summed, on_chip(own), on_chip(other))
    parts = exchange(result.reshape(16, 64, 256), ("y", "c"))
    got = [on_chip(a) for a in (here, far_ahead, far_behind, ahead, behind)]
    halves = pl.pallas_call(
        collect_kernel,
        in_specs=[VMEM] * 5,
        out_specs=VMEM,
        out_shape=jax.ShapeDtypeStruct((ROWS, 64, 256), bf16),
        name="collect",
        compiler_params=LIMIT,
    )(*got)
    halves = swapped(halves)
    out = pl.pallas_call(
        assemble_first_kernel,
        grid=(1,),
        in_specs=[SCALARS] * 2 + [VMEM] * 6,
        out_specs=pl.BlockSpec((1, 64, 4096), lambda i: (0, 0, 0)),
        out_shape=jax.ShapeDtypeStruct((2, 64, 4096), bf16),
        name="assemble_first",
        compiler_params=LIMIT,
    )(at, row, *got, on_chip(halves))
    return pl.pallas_call(
        assemble_second_kernel,
        grid=(2,),
        in_specs=[VMEM, ANY],
        out_specs=pl.BlockSpec((1, 32, 4096), lambda i: (1, i, 0)),
        out_shape=jax.ShapeDtypeStruct((2, 64, 4096), bf16),
        input_output_aliases={1: 0},
        name="assemble_second",
        compiler_params=LIMIT,
    )(on_chip(parts), out)


def solution(mesh):
    fine = Mesh(mesh.devices.reshape(4, 8, 2, 8), ("x", "z", "c", "y"))
    seq = ("x", "z", "c")
    return jax.shard_map(
        program,
        mesh=fine,
        in_specs=(
            P(None, seq, "y"),
            P(None, seq, "y"),
            P(None, seq, "y"),
            P(None, None, "y", seq),
            P(None, "y", None, None),
        ),
        out_specs=P(None, (*seq, "y"), None),
        check_vma=False,
    )
```

```python
import jax
import jax.numpy as jnp
from jax import lax
from jax.experimental import pallas as pl
from jax.experimental.pallas import tpu as pltpu
from jax.sharding import Mesh, PartitionSpec as P


step_size = 0.05
eps_grad = 1e-05
eps_row = 1e-06
f32 = jnp.float32
bf16 = jnp.bfloat16
NT = (((1,), (1,)), ((), ()))
NN = (((1,), (0,)), ((), ()))
ROWS = 8


def dot(a, b, dims):
    return lax.dot_general(a, b, dims, preferred_element_type=f32)


def row_mean(w, i):
    return jnp.mean(w * w, axis=1 if i == 2 else 0, keepdims=True)


def gradients(keys, values, rate_gate, rate_up, rate_down, w_gate, w_up, w_down):
    gate = dot(w_gate, keys, NT)
    up = dot(w_up, keys, NT)
    err = dot(w_down, values, NT)
    sig = jax.nn.sigmoid(gate)
    silu = gate * sig
    hidden = (silu * up).astype(bf16)
    scaled = (hidden.astype(f32) * rate_down).astype(bf16)
    gate_grad = err * up * sig * (1.0 + gate * (1.0 - sig))
    gate_scaled = (gate_grad * rate_gate).astype(bf16)
    up_scaled = (err * silu * rate_up).astype(bf16)
    return (
        dot(gate_scaled, keys, NN),
        dot(up_scaled, keys, NN),
        dot(scaled, values, NN),
    )


def updated(state, targets, grad_ref):
    result = []
    for i in range(3):
        grad = grad_ref[256 * i : 256 * (i + 1), :].astype(f32)
        rms = jnp.sqrt(jnp.mean(grad * grad, keepdims=True) + eps_grad)
        stepped = state[i] + grad * (step_size / rms)
        result.append(stepped * (targets[i] * lax.rsqrt(row_mean(stepped, i) + eps_row)))
    return result


def first_kernel(at, init_ref, k_ref, v_ref, rates_ref, other_ref, own_ref):
    for head, out_ref in ((1 - at[0], other_ref), (at[0], own_ref)):
        cols = pl.ds(pl.multiple_of(head * 256, 256), 256)
        rates = [rates_ref[i, 0, pl.ds(head, 1), :] for i in range(3)]
        weights = [
            jnp.transpose(init_ref[0, head]),
            jnp.transpose(init_ref[1, head]),
            init_ref[2, head],
        ]
        grads = gradients(k_ref[0, :, cols], v_ref[0, :, cols], *rates, *weights)
        for i in range(3):
            out_ref[256 * i : 256 * (i + 1), :] = grads[i].astype(out_ref.dtype)


KEPT = (1032, 256)


def second_kernel(init_ref, grad_ref, own_ref, other_ref, rates_own_ref, rates_other_ref, out_ref, kept_ref):
    init = [init_ref[i].astype(f32) for i in range(3)]
    targets = [jnp.sqrt(row_mean(w, i)) for i, w in enumerate(init)]
    state = updated(init, targets, grad_ref)
    weights = [w.astype(bf16) for w in state]
    for i in range(3):
        kept_ref[256 * i : 256 * (i + 1), :] = state[i]
    kept_ref[768:1024, :] = jnp.broadcast_to(targets[2], (256, 256))
    kept_ref[1024:1025, :] = targets[0]
    kept_ref[1025:1026, :] = targets[1]
    kept_ref[1026:1032, :] = jnp.zeros((6, 256), f32)
    own = gradients(own_ref[0], own_ref[1], *[rates_own_ref[i : i + 1, :] for i in range(3)], *weights)
    other = gradients(other_ref[0], other_ref[1], *[rates_other_ref[i : i + 1, :] for i in range(3)], *weights)
    for i in range(3):
        out_ref[256 * i : 256 * (i + 1), :] = (own[i] + other[i]).astype(bf16)


def state_of(kept_ref):
    return [kept_ref[256 * i : 256 * (i + 1), :] for i in range(3)]


def applied(q, weights):
    gate = dot(q, weights[0], NT)
    up = dot(q, weights[1], NT)
    hidden = (gate * jax.nn.sigmoid(gate) * up).astype(bf16)
    return dot(hidden, weights[2], NN).astype(bf16)


def prepare_kernel(core_ref, k_ref, v_ref, q_ref, init_ref, rates_ref, own_ref, other_ref, w_ref, rates_own_ref, rates_other_ref):
    for head, out_ref, rates_out_ref in (
        (core_ref[0], own_ref, rates_own_ref),
        (1 - core_ref[0], other_ref, rates_other_ref),
    ):
        cols = pl.ds(pl.multiple_of(head * 256, 256), 256)
        out_ref[0] = k_ref[0, :, cols]
        out_ref[1] = v_ref[0, :, cols]
        out_ref[2] = q_ref[1, :, cols]
        out_ref[3] = q_ref[0, :, cols]
        for i in range(3):
            rates_out_ref[i : i + 1, :] = rates_ref[i, 1, pl.ds(head, 1), :]
    for i in range(3):
        w = init_ref[i, core_ref[0]]
        w_ref[i] = w if i == 2 else jnp.transpose(w)


FIRST_LEVEL = ((2, 3, 4), (-3, -2), (1,), (-1,), (0,))
SOURCES = (0, -3, 2, -1, -4, 1, -2, 3)


def apply_first_kernel(row_ref, kept_ref, own_ref, other_ref, *refs):
    outs, scratch = refs[:-1], refs[-1]
    weights = [w.astype(bf16) for w in state_of(kept_ref)]
    for q, side in ((own_ref[3], 0), (other_ref[3], 1)):
        scratch[:, side] = applied(q, weights).reshape(ROWS, 64, 256)
    for ahead, out_ref in zip(FIRST_LEVEL, outs):
        for i, d in enumerate(ahead):
            out_ref[i] = scratch[lax.rem(row_ref[0] + ROWS + d, ROWS)]


def last_kernel(at, kept_ref, grad_ref, own_ref, other_ref, out_ref):
    targets = [kept_ref[1024:1025, :], kept_ref[1025:1026, :], kept_ref[768:1024, :]]
    state = updated(state_of(kept_ref), targets, grad_ref)
    weights = [w.astype(bf16) for w in state]
    for q, core in ((own_ref[2], at[0]), (other_ref[2], 1 - at[0])):
        out_ref[:, pl.ds(core, 1)] = applied(q, weights).reshape(ROWS, 1, 64, 256)


def total_kernel(parts_ref, out_ref):
    total = jnp.sum(parts_ref[...].astype(f32), axis=0, keepdims=True)
    out_ref[...] = jnp.broadcast_to(total.astype(bf16), out_ref.shape)


def pack_kernel(ahead_own_ref, behind_own_ref, far_ahead_ref, far_behind_ref, ahead_ref, behind_ref):
    ahead_ref[0] = ahead_own_ref[0]
    ahead_ref[1] = far_ahead_ref[2]
    behind_ref[0] = behind_own_ref[0]
    behind_ref[1] = far_ahead_ref[0]
    behind_ref[2] = far_behind_ref[0]


def pieces_of(here_ref, far_ahead_ref, far_behind_ref, ahead_ref, behind_ref, side):
    return (
        here_ref[0, side],
        far_ahead_ref[1, side],
        far_behind_ref[1, side],
        ahead_ref[0, side],
        ahead_ref[1, side],
        behind_ref[0, side],
        behind_ref[1, side],
        behind_ref[2, side],
    )


def collect_kernel(*refs):
    for i, piece in enumerate(pieces_of(*refs[:5], 1)):
        refs[5][i] = piece


def assemble_first_kernel(core_ref, row_ref, *refs):
    swapped_ref, out_ref = refs[5], refs[6]
    for i, (source, piece) in enumerate(zip(SOURCES, pieces_of(*refs[:5], 0))):
        first = lax.rem(row_ref[0] + ROWS + source, ROWS) * 512
        own = pl.multiple_of(first + core_ref[0] * 256, 256)
        other = pl.multiple_of(first + (1 - core_ref[0]) * 256, 256)
        out_ref[0, :, pl.ds(own, 256)] = piece
        out_ref[0, :, pl.ds(other, 256)] = swapped_ref[i]


def assemble_second_kernel(parts_ref, prev_ref, out_ref):
    rows = pl.ds(pl.program_id(0) * 32, 32)
    for head in range(16):
        out_ref[0, :, 256 * head : 256 * (head + 1)] = parts_ref[head, rows]


def whole(shape):
    return pl.BlockSpec(shape, lambda i, at: (0,) * len(shape))


def on_chip(array):
    return pltpu.with_memory_space_constraint(array, pltpu.VMEM)


def off_chip(array):
    return pltpu.with_memory_space_constraint(array, pltpu.HBM)


VMEM = pl.BlockSpec(memory_space=pltpu.VMEM)
LIMIT = pltpu.CompilerParams(vmem_limit_bytes=12 << 20)
ANY = pl.BlockSpec(memory_space=pl.ANY)
SCALARS = pl.BlockSpec(memory_space=pltpu.SMEM)


def call(kernel, in_specs, outs, out_specs=None, aliases=None):
    specs = out_specs or [whole(shape) for shape, _ in outs]
    shapes = [jax.ShapeDtypeStruct(shape, dtype) for shape, dtype in outs]
    if len(outs) == 1:
        specs, shapes = specs[0], shapes[0]
    return pl.pallas_call(
        kernel,
        grid_spec=pltpu.PrefetchScalarGridSpec(
            num_scalar_prefetch=1, grid=(1,), in_specs=in_specs, out_specs=specs
        ),
        out_shape=shapes,
        input_output_aliases=aliases or {},
        compiler_params=LIMIT,
    )


def exchange(array, axes):
    return lax.all_to_all(array, axes, split_axis=0, concat_axis=0, tiled=True)


def scattered(partial, block):
    parts = exchange(partial.reshape(32, 24, 256), ("x", "z"))
    return pl.pallas_call(
        total_kernel,
        in_specs=[VMEM],
        out_specs=VMEM,
        out_shape=(pltpu.HBM if block else jax.ShapeDtypeStruct)((32, 24, 256), bf16),
        name="total",
        compiler_params=LIMIT,
    )(on_chip(parts))


def gathered(total):
    full = exchange(total, ("x", "z"))
    return on_chip(full.reshape(768, 256))


def swapped(array):
    return lax.ppermute(array, "c", [(0, 1), (1, 0)])


def program(query_tokens, key_tokens, value_tokens, token_rates, fast_init):
    core = lax.axis_index("c").astype(jnp.int32)
    at = core.reshape(1)
    row = lax.axis_index("y").astype(jnp.int32).reshape(1)

    first_other, first_own = call(
        first_kernel,
        [
            whole((3, 2, 256, 256)),
            pl.BlockSpec((1, 512, 512), lambda i, at: (0, 0, 0)),
            pl.BlockSpec((1, 512, 512), lambda i, at: (0, 0, 0)),
            whole((3, 2, 2, 512)),
        ],
        [((768, 256), bf16), ((768, 256), f32)],
    )(at, *[off_chip(a) for a in (fast_init, key_tokens, value_tokens, token_rates)])
    first_got = swapped(first_other)
    first = (first_own + first_got.astype(f32)).astype(bf16)
    first, query_tokens, key_tokens, value_tokens, token_rates, fast_init = lax.optimization_barrier(
        (first, query_tokens, key_tokens, value_tokens, token_rates, fast_init)
    )

    tokens = (4, 512, 256)
    own, other, init, rates_own, rates_other = call(
        prepare_kernel,
        [
            pl.BlockSpec((1, 512, 512), lambda i, at: (1, 0, 0)),
            pl.BlockSpec((1, 512, 512), lambda i, at: (1, 0, 0)),
            whole((2, 512, 512)),
            whole((3, 2, 256, 256)),
            whole((3, 2, 2, 512)),
        ],
        [(tokens, bf16), (tokens, bf16), ((3, 256, 256), bf16), ((3, 512), f32), ((3, 512), f32)],
    )(at, *[off_chip(a) for a in (key_tokens, value_tokens, query_tokens, fast_init, token_rates)])
    other = swapped(other)
    rates_other = swapped(rates_other)

    total = scattered(first, 0)
    total, other, rates_other, own, rates_own, init = lax.optimization_barrier(
        (total, other, rates_other, own, rates_own, init)
    )
    summed = gathered(total)
    second, kept = pl.pallas_call(
        second_kernel,
        in_specs=[VMEM] * 6,
        out_specs=[VMEM] * 2,
        out_shape=[
            pltpu.HBM((768, 256), bf16),
            jax.ShapeDtypeStruct(KEPT, f32),
        ],
        name="second",
        compiler_params=LIMIT,
    )(on_chip(init), summed, on_chip(own), on_chip(other), rates_own, rates_other)

    far_ahead, far_behind, ahead, behind, here = pl.pallas_call(
        apply_first_kernel,
        in_specs=[SCALARS, VMEM, VMEM, VMEM],
        out_specs=[VMEM] * len(FIRST_LEVEL),
        out_shape=[
            (pltpu.HBM if len(d) == 1 else jax.ShapeDtypeStruct)((len(d), 2, 64, 256), bf16)
            for d in FIRST_LEVEL
        ],
        scratch_shapes=[pltpu.VMEM((ROWS, 2, 64, 256), bf16)],
        name="apply_first",
        compiler_params=LIMIT,
    )(row, on_chip(kept), on_chip(own), on_chip(other))

    def sent(array, step):
        return lax.ppermute(array, "y", [(j, (j + step) % ROWS) for j in range(ROWS)])

    far_ahead = sent(far_ahead, 3)
    far_behind = sent(far_behind, -2)
    ahead, behind = pl.pallas_call(
        pack_kernel,
        in_specs=[VMEM] * 4,
        out_specs=[VMEM] * 2,
        out_shape=[pltpu.HBM((n, 2, 64, 256), bf16) for n in (2, 3)],
        name="pack",
        compiler_params=LIMIT,
    )(*[off_chip(a) for a in (ahead, behind)], *[on_chip(a) for a in (far_ahead, far_behind)])
    ahead = sent(ahead, 1)
    behind = sent(behind, -1)

    total = scattered(second, 1)
    summed = gathered(total)
    result = call(
        last_kernel, [VMEM, VMEM, VMEM, VMEM], [((ROWS, 2, 64, 256), bf16)]
    )(at, on_chip(kept), summed, on_chip(own), on_chip(other))
    parts = exchange(result.reshape(16, 64, 256), ("y", "c"))
    got = [off_chip(here)] + [on_chip(a) for a in (far_ahead, far_behind, ahead, behind)]
    halves = pl.pallas_call(
        collect_kernel,
        in_specs=[VMEM] * 5,
        out_specs=VMEM,
        out_shape=jax.ShapeDtypeStruct((ROWS, 64, 256), bf16),
        name="collect",
        compiler_params=LIMIT,
    )(*got)
    halves = swapped(halves)
    out = pl.pallas_call(
        assemble_first_kernel,
        grid=(1,),
        in_specs=[SCALARS] * 2 + [VMEM] * 6,
        out_specs=pl.BlockSpec((1, 64, 4096), lambda i: (0, 0, 0)),
        out_shape=jax.ShapeDtypeStruct((2, 64, 4096), bf16),
        name="assemble_first",
        compiler_params=LIMIT,
    )(at, row, *got, on_chip(halves))
    return pl.pallas_call(
        assemble_second_kernel,
        grid=(2,),
        in_specs=[VMEM, ANY],
        out_specs=pl.BlockSpec((1, 32, 4096), lambda i: (1, i, 0)),
        out_shape=jax.ShapeDtypeStruct((2, 64, 4096), bf16),
        input_output_aliases={1: 0},
        name="assemble_second",
        compiler_params=LIMIT,
    )(on_chip(parts), out)


def solution(mesh):
    fine = Mesh(mesh.devices.reshape(4, 8, 2, 8), ("x", "z", "c", "y"))
    seq = ("x", "z", "c")
    return jax.shard_map(
        program,
        mesh=fine,
        in_specs=(
            P(None, seq, "y"),
            P(None, seq, "y"),
            P(None, seq, "y"),
            P(None, None, "y", seq),
            P(None, "y", None, None),
        ),
        out_specs=P(None, (*seq, "y"), None),
        check_vma=False,
    )
```

```python
import jax
import jax.numpy as jnp
from jax import lax
from jax.experimental import pallas as pl
from jax.experimental.pallas import tpu as pltpu
from jax.sharding import Mesh, PartitionSpec as P


step_size = 0.05
eps_grad = 1e-05
eps_row = 1e-06
f32 = jnp.float32
bf16 = jnp.bfloat16
NT = (((1,), (1,)), ((), ()))
NN = (((1,), (0,)), ((), ()))
ROWS = 8


def dot(a, b, dims):
    return lax.dot_general(a, b, dims, preferred_element_type=f32)


def row_mean(w, i):
    return jnp.mean(w * w, axis=1 if i == 2 else 0, keepdims=True)


def gradients(keys, values, rate_gate, rate_up, rate_down, w_gate, w_up, w_down):
    gate = dot(w_gate, keys, NT)
    up = dot(w_up, keys, NT)
    err = dot(w_down, values, NT)
    sig = jax.nn.sigmoid(gate)
    silu = gate * sig
    hidden = (silu * up).astype(bf16)
    scaled = (hidden.astype(f32) * rate_down).astype(bf16)
    gate_grad = err * up * sig * (1.0 + gate * (1.0 - sig))
    gate_scaled = (gate_grad * rate_gate).astype(bf16)
    up_scaled = (err * silu * rate_up).astype(bf16)
    return (
        dot(gate_scaled, keys, NN),
        dot(up_scaled, keys, NN),
        dot(scaled, values, NN),
    )


def updated(state, targets, grad_ref):
    result = []
    for i in range(3):
        grad = grad_ref[256 * i : 256 * (i + 1), :].astype(f32)
        rms = jnp.sqrt(jnp.mean(grad * grad, keepdims=True) + eps_grad)
        stepped = state[i] + grad * (step_size / rms)
        result.append(stepped * (targets[i] * lax.rsqrt(row_mean(stepped, i) + eps_row)))
    return result


def first_kernel(at, init_ref, k_ref, v_ref, rates_ref, other_ref, own_ref):
    for head, out_ref in ((1 - at[0], other_ref), (at[0], own_ref)):
        cols = pl.ds(pl.multiple_of(head * 256, 256), 256)
        rates = [rates_ref[i, 0, pl.ds(head, 1), :] for i in range(3)]
        weights = [
            jnp.transpose(init_ref[0, head]),
            jnp.transpose(init_ref[1, head]),
            init_ref[2, head],
        ]
        grads = gradients(k_ref[0, :, cols], v_ref[0, :, cols], *rates, *weights)
        for i in range(3):
            out_ref[256 * i : 256 * (i + 1), :] = grads[i].astype(out_ref.dtype)


KEPT = (1032, 256)


def second_kernel(init_ref, grad_ref, own_ref, other_ref, rates_own_ref, rates_other_ref, out_ref, kept_ref):
    init = [init_ref[i].astype(f32) for i in range(3)]
    targets = [jnp.sqrt(row_mean(w, i)) for i, w in enumerate(init)]
    state = updated(init, targets, grad_ref)
    weights = [w.astype(bf16) for w in state]
    for i in range(3):
        kept_ref[256 * i : 256 * (i + 1), :] = state[i]
    kept_ref[768:1024, :] = jnp.broadcast_to(targets[2], (256, 256))
    kept_ref[1024:1025, :] = targets[0]
    kept_ref[1025:1026, :] = targets[1]
    kept_ref[1026:1032, :] = jnp.zeros((6, 256), f32)
    own = gradients(own_ref[0], own_ref[1], *[rates_own_ref[i : i + 1, :] for i in range(3)], *weights)
    other = gradients(other_ref[0], other_ref[1], *[rates_other_ref[i : i + 1, :] for i in range(3)], *weights)
    for i in range(3):
        out_ref[256 * i : 256 * (i + 1), :] = (own[i] + other[i]).astype(bf16)


def state_of(kept_ref):
    return [kept_ref[256 * i : 256 * (i + 1), :] for i in range(3)]


def applied(q, weights):
    gate = dot(q, weights[0], NT)
    up = dot(q, weights[1], NT)
    hidden = (gate * jax.nn.sigmoid(gate) * up).astype(bf16)
    return dot(hidden, weights[2], NN).astype(bf16)


def prepare_kernel(core_ref, k_ref, v_ref, q_ref, init_ref, rates_ref, own_ref, other_ref, w_ref, rates_own_ref, rates_other_ref):
    for head, out_ref, rates_out_ref in (
        (core_ref[0], own_ref, rates_own_ref),
        (1 - core_ref[0], other_ref, rates_other_ref),
    ):
        cols = pl.ds(pl.multiple_of(head * 256, 256), 256)
        out_ref[0] = k_ref[0, :, cols]
        out_ref[1] = v_ref[0, :, cols]
        out_ref[2] = q_ref[1, :, cols]
        out_ref[3] = q_ref[0, :, cols]
        for i in range(3):
            rates_out_ref[i : i + 1, :] = rates_ref[i, 1, pl.ds(head, 1), :]
    for i in range(3):
        w = init_ref[i, core_ref[0]]
        w_ref[i] = w if i == 2 else jnp.transpose(w)


FIRST_LEVEL = ((2, 3, 4), (-3, -2), (1,), (-1,), (0,))
SOURCES = (0, -3, 2, -1, -4, 1, -2, 3)


def apply_first_kernel(row_ref, kept_ref, own_ref, other_ref, *refs):
    outs, scratch = refs[:-1], refs[-1]
    weights = [w.astype(bf16) for w in state_of(kept_ref)]
    for q, side in ((own_ref[3], 0), (other_ref[3], 1)):
        scratch[:, side] = applied(q, weights).reshape(ROWS, 64, 256)
    for ahead, out_ref in zip(FIRST_LEVEL, outs):
        for i, d in enumerate(ahead):
            out_ref[i] = scratch[lax.rem(row_ref[0] + ROWS + d, ROWS)]


def last_kernel(at, kept_ref, grad_ref, own_ref, other_ref, out_ref):
    targets = [kept_ref[1024:1025, :], kept_ref[1025:1026, :], kept_ref[768:1024, :]]
    state = updated(state_of(kept_ref), targets, grad_ref)
    weights = [w.astype(bf16) for w in state]
    for q, core in ((own_ref[2], at[0]), (other_ref[2], 1 - at[0])):
        out_ref[:, pl.ds(core, 1)] = applied(q, weights).reshape(ROWS, 1, 64, 256)


def total_kernel(parts_ref, out_ref):
    total = jnp.sum(parts_ref[...].astype(f32), axis=0, keepdims=True)
    out_ref[...] = jnp.broadcast_to(total.astype(bf16), out_ref.shape)


def pieces_of(here_ref, far_ahead_ref, far_behind_ref, ahead_ref, behind_ref, side):
    return (
        here_ref[0, side],
        far_ahead_ref[1, side],
        far_behind_ref[1, side],
        ahead_ref[0, side],
        ahead_ref[1, side],
        behind_ref[0, side],
        behind_ref[1, side],
        behind_ref[2, side],
    )


def collect_kernel(*refs):
    for i, piece in enumerate(pieces_of(*refs[:5], 1)):
        refs[5][i] = piece


def assemble_first_kernel(core_ref, row_ref, *refs):
    swapped_ref, out_ref = refs[5], refs[6]
    for i, (source, piece) in enumerate(zip(SOURCES, pieces_of(*refs[:5], 0))):
        first = lax.rem(row_ref[0] + ROWS + source, ROWS) * 512
        own = pl.multiple_of(first + core_ref[0] * 256, 256)
        other = pl.multiple_of(first + (1 - core_ref[0]) * 256, 256)
        out_ref[0, :, pl.ds(own, 256)] = piece
        out_ref[0, :, pl.ds(other, 256)] = swapped_ref[i]


def assemble_second_kernel(parts_ref, prev_ref, out_ref):
    rows = pl.ds(pl.program_id(0) * 32, 32)
    for head in range(16):
        out_ref[0, :, 256 * head : 256 * (head + 1)] = parts_ref[head, rows]


def whole(shape):
    return pl.BlockSpec(shape, lambda i, at: (0,) * len(shape))


def on_chip(array):
    return pltpu.with_memory_space_constraint(array, pltpu.VMEM)


def off_chip(array):
    return pltpu.with_memory_space_constraint(array, pltpu.HBM)


VMEM = pl.BlockSpec(memory_space=pltpu.VMEM)
LIMIT = pltpu.CompilerParams(vmem_limit_bytes=12 << 20)
ANY = pl.BlockSpec(memory_space=pl.ANY)
SCALARS = pl.BlockSpec(memory_space=pltpu.SMEM)


def call(kernel, in_specs, outs, out_specs=None, aliases=None):
    specs = out_specs or [whole(shape) for shape, _ in outs]
    shapes = [jax.ShapeDtypeStruct(shape, dtype) for shape, dtype in outs]
    if len(outs) == 1:
        specs, shapes = specs[0], shapes[0]
    return pl.pallas_call(
        kernel,
        grid_spec=pltpu.PrefetchScalarGridSpec(
            num_scalar_prefetch=1, grid=(1,), in_specs=in_specs, out_specs=specs
        ),
        out_shape=shapes,
        input_output_aliases=aliases or {},
        compiler_params=LIMIT,
    )


def exchange(array, axes):
    return lax.all_to_all(array, axes, split_axis=0, concat_axis=0, tiled=True)


def scattered(partial):
    parts = exchange(partial.reshape(32, 24, 256), ("x", "z"))
    return pl.pallas_call(
        total_kernel,
        in_specs=[VMEM],
        out_specs=VMEM,
        out_shape=jax.ShapeDtypeStruct((32, 24, 256), bf16),
        name="total",
        compiler_params=LIMIT,
    )(on_chip(parts))


def gathered(total):
    full = exchange(total, ("x", "z"))
    return on_chip(full.reshape(768, 256))


def swapped(array):
    return lax.ppermute(array, "c", [(0, 1), (1, 0)])


def program(query_tokens, key_tokens, value_tokens, token_rates, fast_init):
    core = lax.axis_index("c").astype(jnp.int32)
    at = core.reshape(1)
    row = lax.axis_index("y").astype(jnp.int32).reshape(1)

    first_other, first_own = call(
        first_kernel,
        [
            whole((3, 2, 256, 256)),
            pl.BlockSpec((1, 512, 512), lambda i, at: (0, 0, 0)),
            pl.BlockSpec((1, 512, 512), lambda i, at: (0, 0, 0)),
            whole((3, 2, 2, 512)),
        ],
        [((768, 256), bf16), ((768, 256), f32)],
    )(at, *[off_chip(a) for a in (fast_init, key_tokens, value_tokens, token_rates)])
    first_got = swapped(first_other)
    first = (first_own + first_got.astype(f32)).astype(bf16)
    first, query_tokens, key_tokens, value_tokens, token_rates, fast_init = lax.optimization_barrier(
        (first, query_tokens, key_tokens, value_tokens, token_rates, fast_init)
    )

    tokens = (4, 512, 256)
    own, other, init, rates_own, rates_other = call(
        prepare_kernel,
        [
            pl.BlockSpec((1, 512, 512), lambda i, at: (1, 0, 0)),
            pl.BlockSpec((1, 512, 512), lambda i, at: (1, 0, 0)),
            whole((2, 512, 512)),
            whole((3, 2, 256, 256)),
            whole((3, 2, 2, 512)),
        ],
        [(tokens, bf16), (tokens, bf16), ((3, 256, 256), bf16), ((3, 512), f32), ((3, 512), f32)],
    )(at, *[off_chip(a) for a in (key_tokens, value_tokens, query_tokens, fast_init, token_rates)])
    other = swapped(other)
    rates_other = swapped(rates_other)

    total = scattered(first)
    total, other, rates_other, own, rates_own, init = lax.optimization_barrier(
        (total, other, rates_other, own, rates_own, init)
    )
    summed = gathered(total)
    second, kept = pl.pallas_call(
        second_kernel,
        in_specs=[VMEM] * 6,
        out_specs=[VMEM] * 2,
        out_shape=[
            pltpu.HBM((768, 256), bf16),
            jax.ShapeDtypeStruct(KEPT, f32),
        ],
        name="second",
        compiler_params=LIMIT,
    )(on_chip(init), summed, on_chip(own), on_chip(other), rates_own, rates_other)

    far_ahead, far_behind, ahead, behind, here = pl.pallas_call(
        apply_first_kernel,
        in_specs=[SCALARS, VMEM, VMEM, VMEM],
        out_specs=[VMEM] * len(FIRST_LEVEL),
        out_shape=[
            (pltpu.HBM if i > 1 else jax.ShapeDtypeStruct)((n, 2, 64, 256), bf16) for i, n in enumerate((3, 2, 2, 3, 1))
        ],
        scratch_shapes=[pltpu.VMEM((ROWS, 2, 64, 256), bf16)],
        name="apply_first",
        compiler_params=LIMIT,
    )(row, on_chip(kept), on_chip(own), on_chip(other))

    def sent(array, step):
        return lax.ppermute(array, "y", [(j, (j + step) % ROWS) for j in range(ROWS)])

    far_ahead = sent(far_ahead, 3)
    far_behind = sent(far_behind, -2)
    ahead = sent(lax.dynamic_update_slice(ahead, far_ahead[2:], (1, 0, 0, 0)), 1)
    behind = lax.dynamic_update_slice(behind, far_ahead[:1], (1, 0, 0, 0))
    behind = sent(lax.dynamic_update_slice(behind, far_behind[:1], (2, 0, 0, 0)), -1)

    total = scattered(second)
    summed = gathered(total)
    result = call(
        last_kernel, [VMEM, VMEM, VMEM, VMEM], [((ROWS, 2, 64, 256), bf16)]
    )(at, on_chip(kept), summed, on_chip(own), on_chip(other))
    parts = exchange(result.reshape(16, 64, 256), ("y", "c"))
    got = [on_chip(a) for a in (here, far_ahead, far_behind, ahead, behind)]
    halves = pl.pallas_call(
        collect_kernel,
        in_specs=[VMEM] * 5,
        out_specs=VMEM,
        out_shape=jax.ShapeDtypeStruct((ROWS, 64, 256), bf16),
        name="collect",
        compiler_params=LIMIT,
    )(*got)
    halves = swapped(halves)
    out = pl.pallas_call(
        assemble_first_kernel,
        grid=(1,),
        in_specs=[SCALARS] * 2 + [VMEM] * 6,
        out_specs=pl.BlockSpec((1, 64, 4096), lambda i: (0, 0, 0)),
        out_shape=jax.ShapeDtypeStruct((2, 64, 4096), bf16),
        name="assemble_first",
        compiler_params=LIMIT,
    )(at, row, *got, on_chip(halves))
    return pl.pallas_call(
        assemble_second_kernel,
        grid=(2,),
        in_specs=[VMEM, ANY],
        out_specs=pl.BlockSpec((1, 32, 4096), lambda i: (1, i, 0)),
        out_shape=jax.ShapeDtypeStruct((2, 64, 4096), bf16),
        input_output_aliases={1: 0},
        name="assemble_second",
        compiler_params=LIMIT,
    )(on_chip(parts), out)


def solution(mesh):
    fine = Mesh(mesh.devices.reshape(4, 8, 2, 8), ("x", "z", "c", "y"))
    seq = ("x", "z", "c")
    return jax.shard_map(
        program,
        mesh=fine,
        in_specs=(
            P(None, seq, "y"),
            P(None, seq, "y"),
            P(None, seq, "y"),
            P(None, None, "y", seq),
            P(None, "y", None, None),
        ),
        out_specs=P(None, (*seq, "y"), None),
        check_vma=False,
    )
```

```python
import jax
import jax.numpy as jnp
from jax import lax
from jax.experimental import pallas as pl
from jax.experimental.pallas import tpu as pltpu
from jax.sharding import Mesh, PartitionSpec as P


step_size = 0.05
eps_grad = 1e-05
eps_row = 1e-06
f32 = jnp.float32
bf16 = jnp.bfloat16
NT = (((1,), (1,)), ((), ()))
NN = (((1,), (0,)), ((), ()))
ROWS = 8


def dot(a, b, dims):
    return lax.dot_general(a, b, dims, preferred_element_type=f32)


def row_mean(w, i):
    return jnp.mean(w * w, axis=1 if i == 2 else 0, keepdims=True)


def gradients(keys, values, rate_gate, rate_up, rate_down, w_gate, w_up, w_down):
    gate = dot(w_gate, keys, NT)
    up = dot(w_up, keys, NT)
    err = dot(w_down, values, NT)
    sig = jax.nn.sigmoid(gate)
    silu = gate * sig
    hidden = (silu * up).astype(bf16)
    scaled = (hidden.astype(f32) * rate_down).astype(bf16)
    gate_grad = err * up * sig * (1.0 + gate * (1.0 - sig))
    gate_scaled = (gate_grad * rate_gate).astype(bf16)
    up_scaled = (err * silu * rate_up).astype(bf16)
    return (
        dot(gate_scaled, keys, NN),
        dot(up_scaled, keys, NN),
        dot(scaled, values, NN),
    )


def updated(state, targets, grad_ref):
    result = []
    for i in range(3):
        grad = grad_ref[256 * i : 256 * (i + 1), :].astype(f32)
        rms = jnp.sqrt(jnp.mean(grad * grad, keepdims=True) + eps_grad)
        stepped = state[i] + grad * (step_size / rms)
        result.append(stepped * (targets[i] * lax.rsqrt(row_mean(stepped, i) + eps_row)))
    return result


def first_kernel(at, init_ref, k_ref, v_ref, rates_ref, other_ref, own_ref):
    for head, out_ref in ((1 - at[0], other_ref), (at[0], own_ref)):
        cols = pl.ds(pl.multiple_of(head * 256, 256), 256)
        rates = [rates_ref[i, 0, pl.ds(head, 1), :] for i in range(3)]
        weights = [
            jnp.transpose(init_ref[0, head]),
            jnp.transpose(init_ref[1, head]),
            init_ref[2, head],
        ]
        grads = gradients(k_ref[0, :, cols], v_ref[0, :, cols], *rates, *weights)
        for i in range(3):
            out_ref[256 * i : 256 * (i + 1), :] = grads[i].astype(out_ref.dtype)


KEPT = (1032, 256)


def second_kernel(init_ref, grad_ref, own_ref, other_ref, rates_own_ref, rates_other_ref, out_ref, kept_ref):
    init = [init_ref[i].astype(f32) for i in range(3)]
    targets = [jnp.sqrt(row_mean(w, i)) for i, w in enumerate(init)]
    state = updated(init, targets, grad_ref)
    weights = [w.astype(bf16) for w in state]
    for i in range(3):
        kept_ref[256 * i : 256 * (i + 1), :] = state[i]
    kept_ref[768:1024, :] = jnp.broadcast_to(targets[2], (256, 256))
    kept_ref[1024:1025, :] = targets[0]
    kept_ref[1025:1026, :] = targets[1]
    kept_ref[1026:1032, :] = jnp.zeros((6, 256), f32)
    own = gradients(own_ref[0], own_ref[1], *[rates_own_ref[i : i + 1, :] for i in range(3)], *weights)
    other = gradients(other_ref[0], other_ref[1], *[rates_other_ref[i : i + 1, :] for i in range(3)], *weights)
    for i in range(3):
        out_ref[256 * i : 256 * (i + 1), :] = (own[i] + other[i]).astype(bf16)


def state_of(kept_ref):
    return [kept_ref[256 * i : 256 * (i + 1), :] for i in range(3)]


def applied(q, weights):
    gate = dot(q, weights[0], NT)
    up = dot(q, weights[1], NT)
    hidden = (gate * jax.nn.sigmoid(gate) * up).astype(bf16)
    return dot(hidden, weights[2], NN).astype(bf16)


def prepare_kernel(core_ref, k_ref, v_ref, q_ref, init_ref, rates_ref, own_ref, other_ref, w_ref, rates_own_ref, rates_other_ref):
    for head, out_ref, rates_out_ref in (
        (core_ref[0], own_ref, rates_own_ref),
        (1 - core_ref[0], other_ref, rates_other_ref),
    ):
        cols = pl.ds(pl.multiple_of(head * 256, 256), 256)
        out_ref[0] = k_ref[0, :, cols]
        out_ref[1] = v_ref[0, :, cols]
        out_ref[2] = q_ref[1, :, cols]
        out_ref[3] = q_ref[0, :, cols]
        for i in range(3):
            rates_out_ref[i : i + 1, :] = rates_ref[i, 1, pl.ds(head, 1), :]
    for i in range(3):
        w = init_ref[i, core_ref[0]]
        w_ref[i] = w if i == 2 else jnp.transpose(w)


FIRST_LEVEL = ((2, 3, 4), (-3, -2), (1,), (-1,), (0,))
SOURCES = (0, -3, 2, -1, -4, 1, -2, 3)


def apply_first_kernel(row_ref, kept_ref, own_ref, other_ref, *refs):
    outs, scratch = refs[:-1], refs[-1]
    weights = [w.astype(bf16) for w in state_of(kept_ref)]
    for q, side in ((own_ref[3], 0), (other_ref[3], 1)):
        scratch[:, side] = applied(q, weights).reshape(ROWS, 64, 256)
    for ahead, out_ref in zip(FIRST_LEVEL, outs):
        for i, d in enumerate(ahead):
            out_ref[i] = scratch[lax.rem(row_ref[0] + ROWS + d, ROWS)]


def last_kernel(at, kept_ref, grad_ref, own_ref, other_ref, out_ref):
    targets = [kept_ref[1024:1025, :], kept_ref[1025:1026, :], kept_ref[768:1024, :]]
    state = updated(state_of(kept_ref), targets, grad_ref)
    weights = [w.astype(bf16) for w in state]
    for q, core in ((own_ref[2], at[0]), (other_ref[2], 1 - at[0])):
        out_ref[:, pl.ds(core, 1)] = applied(q, weights).reshape(ROWS, 1, 64, 256)


def total_with_rates_kernel(parts_ref, rates_ref, out_ref, rates_out_ref):
    rates_out_ref[...] = rates_ref[...]
    total_kernel(parts_ref, out_ref)


def total_kernel(parts_ref, out_ref):
    total = jnp.sum(parts_ref[...].astype(f32), axis=0, keepdims=True)
    out_ref[...] = jnp.broadcast_to(total.astype(bf16), out_ref.shape)


def pieces_of(here_ref, far_ahead_ref, far_behind_ref, ahead_ref, behind_ref, side):
    return (
        here_ref[0, side],
        far_ahead_ref[1, side],
        far_behind_ref[1, side],
        ahead_ref[0, side],
        ahead_ref[1, side],
        behind_ref[0, side],
        behind_ref[1, side],
        behind_ref[2, side],
    )


def collect_kernel(*refs):
    for i, piece in enumerate(pieces_of(*refs[:5], 1)):
        refs[5][i] = piece


def assemble_first_kernel(core_ref, row_ref, *refs):
    swapped_ref, out_ref = refs[5], refs[6]
    for i, (source, piece) in enumerate(zip(SOURCES, pieces_of(*refs[:5], 0))):
        first = lax.rem(row_ref[0] + ROWS + source, ROWS) * 512
        own = pl.multiple_of(first + core_ref[0] * 256, 256)
        other = pl.multiple_of(first + (1 - core_ref[0]) * 256, 256)
        out_ref[0, :, pl.ds(own, 256)] = piece
        out_ref[0, :, pl.ds(other, 256)] = swapped_ref[i]


def assemble_second_kernel(parts_ref, prev_ref, out_ref):
    rows = pl.ds(pl.program_id(0) * 32, 32)
    for head in range(16):
        out_ref[0, :, 256 * head : 256 * (head + 1)] = parts_ref[head, rows]


def whole(shape):
    return pl.BlockSpec(shape, lambda i, at: (0,) * len(shape))


def on_chip(array):
    return pltpu.with_memory_space_constraint(array, pltpu.VMEM)


def off_chip(array):
    return pltpu.with_memory_space_constraint(array, pltpu.HBM)


VMEM = pl.BlockSpec(memory_space=pltpu.VMEM)
LIMIT = pltpu.CompilerParams(vmem_limit_bytes=12 << 20)
ANY = pl.BlockSpec(memory_space=pl.ANY)
SCALARS = pl.BlockSpec(memory_space=pltpu.SMEM)


def call(kernel, in_specs, outs, out_specs=None, aliases=None):
    specs = out_specs or [whole(shape) for shape, _ in outs]
    shapes = [jax.ShapeDtypeStruct(shape, dtype) for shape, dtype in outs]
    if len(outs) == 1:
        specs, shapes = specs[0], shapes[0]
    return pl.pallas_call(
        kernel,
        grid_spec=pltpu.PrefetchScalarGridSpec(
            num_scalar_prefetch=1, grid=(1,), in_specs=in_specs, out_specs=specs
        ),
        out_shape=shapes,
        input_output_aliases=aliases or {},
        compiler_params=LIMIT,
    )


def exchange(array, axes):
    return lax.all_to_all(array, axes, split_axis=0, concat_axis=0, tiled=True)


def scattered(partial, rates=None):
    parts = exchange(partial.reshape(32, 24, 256), ("x", "z"))
    args = [on_chip(parts)] if rates is None else [on_chip(parts), on_chip(rates)]
    shapes = [jax.ShapeDtypeStruct((32, 24, 256), bf16), jax.ShapeDtypeStruct((3, 512), f32)][: len(args)]
    result = pl.pallas_call(
        total_kernel if rates is None else total_with_rates_kernel,
        in_specs=[VMEM] * len(args),
        out_specs=[VMEM] * len(args),
        out_shape=shapes,
        name="total",
        compiler_params=LIMIT,
    )(*args)
    return result[0] if rates is None else result


def gathered(total):
    full = exchange(total, ("x", "z"))
    return on_chip(full.reshape(768, 256))


def swapped(array):
    return lax.ppermute(array, "c", [(0, 1), (1, 0)])


def program(query_tokens, key_tokens, value_tokens, token_rates, fast_init):
    core = lax.axis_index("c").astype(jnp.int32)
    at = core.reshape(1)
    row = lax.axis_index("y").astype(jnp.int32).reshape(1)

    first_other, first_own = call(
        first_kernel,
        [
            whole((3, 2, 256, 256)),
            pl.BlockSpec((1, 512, 512), lambda i, at: (0, 0, 0)),
            pl.BlockSpec((1, 512, 512), lambda i, at: (0, 0, 0)),
            whole((3, 2, 2, 512)),
        ],
        [((768, 256), bf16), ((768, 256), f32)],
    )(at, *[off_chip(a) for a in (fast_init, key_tokens, value_tokens, token_rates)])
    first_got = swapped(first_other)
    first = (first_own + first_got.astype(f32)).astype(bf16)
    first, query_tokens, key_tokens, value_tokens, token_rates, fast_init = lax.optimization_barrier(
        (first, query_tokens, key_tokens, value_tokens, token_rates, fast_init)
    )

    tokens = (4, 512, 256)
    own, other, init, rates_own, rates_other = call(
        prepare_kernel,
        [
            pl.BlockSpec((1, 512, 512), lambda i, at: (1, 0, 0)),
            pl.BlockSpec((1, 512, 512), lambda i, at: (1, 0, 0)),
            whole((2, 512, 512)),
            whole((3, 2, 256, 256)),
            whole((3, 2, 2, 512)),
        ],
        [(tokens, bf16), (tokens, bf16), ((3, 256, 256), bf16), ((3, 512), f32), ((3, 512), f32)],
    )(at, *[off_chip(a) for a in (key_tokens, value_tokens, query_tokens, fast_init, token_rates)])
    other = swapped(other)
    rates_other = swapped(rates_other)

    total, rates_other = scattered(first, rates_other)
    total, other, rates_other, own, rates_own, init = lax.optimization_barrier(
        (total, other, rates_other, own, rates_own, init)
    )
    summed = gathered(total)
    second, kept = pl.pallas_call(
        second_kernel,
        in_specs=[VMEM] * 6,
        out_specs=[VMEM] * 2,
        out_shape=[
            pltpu.HBM((768, 256), bf16),
            jax.ShapeDtypeStruct(KEPT, f32),
        ],
        name="second",
        compiler_params=LIMIT,
    )(on_chip(init), summed, on_chip(own), on_chip(other), rates_own, rates_other)

    far_ahead, far_behind, ahead, behind, here = pl.pallas_call(
        apply_first_kernel,
        in_specs=[SCALARS, VMEM, VMEM, VMEM],
        out_specs=[VMEM] * len(FIRST_LEVEL),
        out_shape=[
            (pltpu.HBM if i > 1 else jax.ShapeDtypeStruct)((n, 2, 64, 256), bf16) for i, n in enumerate((3, 2, 2, 3, 1))
        ],
        scratch_shapes=[pltpu.VMEM((ROWS, 2, 64, 256), bf16)],
        name="apply_first",
        compiler_params=LIMIT,
    )(row, on_chip(kept), on_chip(own), on_chip(other))

    def sent(array, step):
        return lax.ppermute(array, "y", [(j, (j + step) % ROWS) for j in range(ROWS)])

    far_ahead = sent(far_ahead, 3)
    far_behind = sent(far_behind, -2)
    ahead = sent(lax.dynamic_update_slice(ahead, far_ahead[2:], (1, 0, 0, 0)), 1)
    behind = lax.dynamic_update_slice(behind, far_ahead[:1], (1, 0, 0, 0))
    behind = sent(lax.dynamic_update_slice(behind, far_behind[:1], (2, 0, 0, 0)), -1)

    total = scattered(second)
    summed = gathered(total)
    result = call(
        last_kernel, [VMEM, VMEM, VMEM, VMEM], [((ROWS, 2, 64, 256), bf16)]
    )(at, on_chip(kept), summed, on_chip(own), on_chip(other))
    parts = exchange(result.reshape(16, 64, 256), ("y", "c"))
    got = [off_chip(here)] + [on_chip(a) for a in (far_ahead, far_behind, ahead, behind)]
    halves = pl.pallas_call(
        collect_kernel,
        in_specs=[VMEM] * 5,
        out_specs=VMEM,
        out_shape=jax.ShapeDtypeStruct((ROWS, 64, 256), bf16),
        name="collect",
        compiler_params=LIMIT,
    )(*got)
    halves = swapped(halves)
    out = pl.pallas_call(
        assemble_first_kernel,
        grid=(1,),
        in_specs=[SCALARS] * 2 + [VMEM] * 6,
        out_specs=pl.BlockSpec((1, 64, 4096), lambda i: (0, 0, 0)),
        out_shape=jax.ShapeDtypeStruct((2, 64, 4096), bf16),
        name="assemble_first",
        compiler_params=LIMIT,
    )(at, row, *got, on_chip(halves))
    return pl.pallas_call(
        assemble_second_kernel,
        grid=(2,),
        in_specs=[VMEM, ANY],
        out_specs=pl.BlockSpec((1, 32, 4096), lambda i: (1, i, 0)),
        out_shape=jax.ShapeDtypeStruct((2, 64, 4096), bf16),
        input_output_aliases={1: 0},
        name="assemble_second",
        compiler_params=LIMIT,
    )(on_chip(parts), out)


def solution(mesh):
    fine = Mesh(mesh.devices.reshape(4, 8, 2, 8), ("x", "z", "c", "y"))
    seq = ("x", "z", "c")
    return jax.shard_map(
        program,
        mesh=fine,
        in_specs=(
            P(None, seq, "y"),
            P(None, seq, "y"),
            P(None, seq, "y"),
            P(None, None, "y", seq),
            P(None, "y", None, None),
        ),
        out_specs=P(None, (*seq, "y"), None),
        check_vma=False,
    )
```

```python
import jax
import jax.numpy as jnp
from jax import lax
from jax.experimental import pallas as pl
from jax.experimental.pallas import tpu as pltpu
from jax.sharding import Mesh, PartitionSpec as P


step_size = 0.05
eps_grad = 1e-05
eps_row = 1e-06
f32 = jnp.float32
bf16 = jnp.bfloat16
NT = (((1,), (1,)), ((), ()))
NN = (((1,), (0,)), ((), ()))
ROWS = 8


def dot(a, b, dims):
    return lax.dot_general(a, b, dims, preferred_element_type=f32)


def row_mean(w, i):
    return jnp.mean(w * w, axis=1 if i == 2 else 0, keepdims=True)


def scaled_errors(keys, values, rate_gate, rate_up, rate_down, w_gate, w_up, w_down):
    gate = dot(w_gate, keys, NT)
    up = dot(w_up, keys, NT)
    err = dot(w_down, values, NT)
    sig = jax.nn.sigmoid(gate)
    silu = gate * sig
    hidden = (silu * up).astype(bf16)
    scaled = (hidden.astype(f32) * rate_down).astype(bf16)
    gate_grad = err * up * sig * (1.0 + gate * (1.0 - sig))
    gate_scaled = (gate_grad * rate_gate).astype(bf16)
    up_scaled = (err * silu * rate_up).astype(bf16)
    return gate_scaled, up_scaled, scaled


def gradients(keys, values, *rest):
    gate_scaled, up_scaled, scaled = scaled_errors(keys, values, *rest)
    return dot(gate_scaled, keys, NN), dot(up_scaled, keys, NN), dot(scaled, values, NN)


def updated(state, targets, grad_ref):
    result = []
    for i in range(3):
        grad = grad_ref[256 * i : 256 * (i + 1), :].astype(f32)
        rms = jnp.sqrt(jnp.mean(grad * grad, keepdims=True) + eps_grad)
        stepped = state[i] + grad * (step_size / rms)
        result.append(stepped * (targets[i] * lax.rsqrt(row_mean(stepped, i) + eps_row)))
    return result


def first_kernel(at, init_ref, k_ref, v_ref, rates_ref, other_ref, own_ref):
    for head, out_ref in ((1 - at[0], other_ref), (at[0], own_ref)):
        cols = pl.ds(pl.multiple_of(head * 256, 256), 256)
        rates = [rates_ref[i, 0, pl.ds(head, 1), :] for i in range(3)]
        weights = [
            jnp.transpose(init_ref[0, head]),
            jnp.transpose(init_ref[1, head]),
            init_ref[2, head],
        ]
        grads = gradients(k_ref[0, :, cols], v_ref[0, :, cols], *rates, *weights)
        for i in range(3):
            out_ref[256 * i : 256 * (i + 1), :] = grads[i].astype(out_ref.dtype)


KEPT = (1032, 256)


def second_kernel(init_ref, grad_ref, own_ref, other_ref, rates_own_ref, rates_other_ref, out_ref, kept_ref, scratch, sems):
    init = [init_ref[i].astype(f32) for i in range(3)]
    targets = [jnp.sqrt(row_mean(w, i)) for i, w in enumerate(init)]
    state = updated(init, targets, grad_ref)
    weights = [w.astype(bf16) for w in state]
    for i in range(3):
        kept_ref[256 * i : 256 * (i + 1), :] = state[i]
    kept_ref[768:1024, :] = jnp.broadcast_to(targets[2], (256, 256))
    kept_ref[1024:1025, :] = targets[0]
    kept_ref[1025:1026, :] = targets[1]
    kept_ref[1026:1032, :] = jnp.zeros((6, 256), f32)
    halves = (
        (own_ref[0], own_ref[1], [rates_own_ref[i : i + 1, :] for i in range(3)]),
        (other_ref[0], other_ref[1], [rates_other_ref[i : i + 1, :] for i in range(3)]),
    )
    scaled = [scaled_errors(k, v, *rates, *weights) for k, v, rates in halves]
    copies = []
    for i in range(3):
        rows = slice(256 * i, 256 * (i + 1))
        grad = sum(dot(scaled[h][i], halves[h][1 if i == 2 else 0], NN) for h in (0, 1))
        scratch[rows, :] = grad.astype(bf16)
        copies.append(pltpu.make_async_copy(scratch.at[rows], out_ref.at[rows], sems.at[i]))
        copies[-1].start()
    for copy in copies:
        copy.wait()


def state_of(kept_ref):
    return [kept_ref[256 * i : 256 * (i + 1), :] for i in range(3)]


def applied(q, weights):
    gate = dot(q, weights[0], NT)
    up = dot(q, weights[1], NT)
    hidden = (gate * jax.nn.sigmoid(gate) * up).astype(bf16)
    return dot(hidden, weights[2], NN).astype(bf16)


def prepare_kernel(core_ref, k_ref, v_ref, q_ref, init_ref, rates_ref, own_ref, other_ref, w_ref, rates_own_ref, rates_other_ref):
    for head, out_ref, rates_out_ref in (
        (core_ref[0], own_ref, rates_own_ref),
        (1 - core_ref[0], other_ref, rates_other_ref),
    ):
        cols = pl.ds(pl.multiple_of(head * 256, 256), 256)
        out_ref[0] = k_ref[0, :, cols]
        out_ref[1] = v_ref[0, :, cols]
        out_ref[2] = q_ref[1, :, cols]
        out_ref[3] = q_ref[0, :, cols]
        for i in range(3):
            rates_out_ref[i : i + 1, :] = rates_ref[i, 1, pl.ds(head, 1), :]
    for i in range(3):
        w = init_ref[i, core_ref[0]]
        w_ref[i] = w if i == 2 else jnp.transpose(w)


FIRST_LEVEL = ((2, 3, 4), (-3, -2), (1,), (-1,), (0,))
SOURCES = (0, -3, 2, -1, -4, 1, -2, 3)


def apply_first_kernel(row_ref, kept_ref, own_ref, other_ref, *refs):
    outs, scratch = refs[:-1], refs[-1]
    weights = [w.astype(bf16) for w in state_of(kept_ref)]
    for q, side in ((own_ref[3], 0), (other_ref[3], 1)):
        scratch[:, side] = applied(q, weights).reshape(ROWS, 64, 256)
    for ahead, out_ref in zip(FIRST_LEVEL, outs):
        for i, d in enumerate(ahead):
            out_ref[i] = scratch[lax.rem(row_ref[0] + ROWS + d, ROWS)]


def last_kernel(at, kept_ref, grad_ref, own_ref, other_ref, out_ref, scratch, sems):
    targets = [kept_ref[1024:1025, :], kept_ref[1025:1026, :], kept_ref[768:1024, :]]
    state = updated(state_of(kept_ref), targets, grad_ref)
    weights = [w.astype(bf16) for w in state]
    copies = []
    for side, (q, core) in enumerate(((own_ref[2], at[0]), (other_ref[2], 1 - at[0]))):
        scratch[side] = applied(q, weights).reshape(ROWS, 64, 256)
        copies.append(pltpu.make_async_copy(scratch.at[side], out_ref.at[:, core], sems.at[side]))
        copies[-1].start()
    for copy in copies:
        copy.wait()


def total_with_rates_kernel(parts_ref, rates_ref, out_ref, rates_out_ref):
    rates_out_ref[...] = rates_ref[...]
    total_kernel(parts_ref, out_ref)


def total_kernel(parts_ref, out_ref):
    total = jnp.sum(parts_ref[...].astype(f32), axis=0, keepdims=True)
    out_ref[...] = jnp.broadcast_to(total.astype(bf16), out_ref.shape)


def pieces_of(here_ref, far_ahead_ref, far_behind_ref, ahead_ref, behind_ref, side):
    return (
        here_ref[0, side],
        far_ahead_ref[1, side],
        far_behind_ref[1, side],
        ahead_ref[0, side],
        ahead_ref[1, side],
        behind_ref[0, side],
        behind_ref[1, side],
        behind_ref[2, side],
    )


def collect_kernel(*refs):
    for i, piece in enumerate(pieces_of(*refs[:5], 1)):
        refs[5][i] = piece


def assemble_first_kernel(core_ref, row_ref, *refs):
    swapped_ref, out_ref = refs[5], refs[6]
    for i, (source, piece) in enumerate(zip(SOURCES, pieces_of(*refs[:5], 0))):
        first = lax.rem(row_ref[0] + ROWS + source, ROWS) * 512
        own = pl.multiple_of(first + core_ref[0] * 256, 256)
        other = pl.multiple_of(first + (1 - core_ref[0]) * 256, 256)
        out_ref[0, :, pl.ds(own, 256)] = piece
        out_ref[0, :, pl.ds(other, 256)] = swapped_ref[i]


def assemble_second_kernel(parts_ref, prev_ref, out_ref):
    rows = pl.ds(pl.program_id(0) * 32, 32)
    for head in range(16):
        out_ref[0, :, 256 * head : 256 * (head + 1)] = parts_ref[head, rows]


def whole(shape):
    return pl.BlockSpec(shape, lambda i, at: (0,) * len(shape))


def on_chip(array):
    return pltpu.with_memory_space_constraint(array, pltpu.VMEM)


def off_chip(array):
    return pltpu.with_memory_space_constraint(array, pltpu.HBM)


VMEM = pl.BlockSpec(memory_space=pltpu.VMEM)
LIMIT = pltpu.CompilerParams(vmem_limit_bytes=12 << 20)
ANY = pl.BlockSpec(memory_space=pl.ANY)
SCALARS = pl.BlockSpec(memory_space=pltpu.SMEM)


def call(kernel, in_specs, outs, out_specs=None, aliases=None):
    specs = out_specs or [whole(shape) for shape, _ in outs]
    shapes = [jax.ShapeDtypeStruct(shape, dtype) for shape, dtype in outs]
    if len(outs) == 1:
        specs, shapes = specs[0], shapes[0]
    return pl.pallas_call(
        kernel,
        grid_spec=pltpu.PrefetchScalarGridSpec(
            num_scalar_prefetch=1, grid=(1,), in_specs=in_specs, out_specs=specs
        ),
        out_shape=shapes,
        input_output_aliases=aliases or {},
        compiler_params=LIMIT,
    )


def exchange(array, axes):
    return lax.all_to_all(array, axes, split_axis=0, concat_axis=0, tiled=True)


def scattered(partial, rates=None):
    parts = exchange(partial.reshape(32, 24, 256), ("x", "z"))
    args = [on_chip(parts)] if rates is None else [on_chip(parts), on_chip(rates)]
    shapes = [jax.ShapeDtypeStruct((32, 24, 256), bf16), jax.ShapeDtypeStruct((3, 512), f32)][: len(args)]
    result = pl.pallas_call(
        total_kernel if rates is None else total_with_rates_kernel,
        in_specs=[VMEM] * len(args),
        out_specs=[VMEM] * len(args),
        out_shape=shapes,
        name="total",
        compiler_params=LIMIT,
    )(*args)
    return result[0] if rates is None else result


def gathered(total):
    full = exchange(total, ("x", "z"))
    return on_chip(full.reshape(768, 256))


def swapped(array):
    return lax.ppermute(array, "c", [(0, 1), (1, 0)])


def program(query_tokens, key_tokens, value_tokens, token_rates, fast_init):
    core = lax.axis_index("c").astype(jnp.int32)
    at = core.reshape(1)
    row = lax.axis_index("y").astype(jnp.int32).reshape(1)

    first_other, first_own = call(
        first_kernel,
        [
            whole((3, 2, 256, 256)),
            pl.BlockSpec((1, 512, 512), lambda i, at: (0, 0, 0)),
            pl.BlockSpec((1, 512, 512), lambda i, at: (0, 0, 0)),
            whole((3, 2, 2, 512)),
        ],
        [((768, 256), bf16), ((768, 256), f32)],
    )(at, *[off_chip(a) for a in (fast_init, key_tokens, value_tokens, token_rates)])
    first_got = swapped(first_other)
    first = (first_own + first_got.astype(f32)).astype(bf16)
    first, query_tokens, key_tokens, value_tokens, token_rates, fast_init = lax.optimization_barrier(
        (first, query_tokens, key_tokens, value_tokens, token_rates, fast_init)
    )

    tokens = (4, 512, 256)
    own, other, init, rates_own, rates_other = call(
        prepare_kernel,
        [
            pl.BlockSpec((1, 512, 512), lambda i, at: (1, 0, 0)),
            pl.BlockSpec((1, 512, 512), lambda i, at: (1, 0, 0)),
            whole((2, 512, 512)),
            whole((3, 2, 256, 256)),
            whole((3, 2, 2, 512)),
        ],
        [(tokens, bf16), (tokens, bf16), ((3, 256, 256), bf16), ((3, 512), f32), ((3, 512), f32)],
    )(at, *[off_chip(a) for a in (key_tokens, value_tokens, query_tokens, fast_init, token_rates)])
    other = swapped(other)
    rates_other = swapped(rates_other)

    total, rates_other = scattered(first, rates_other)
    total, other, rates_other, own, rates_own, init = lax.optimization_barrier(
        (total, other, rates_other, own, rates_own, init)
    )
    summed = gathered(total)
    second, kept = pl.pallas_call(
        second_kernel,
        in_specs=[VMEM] * 6,
        out_specs=[ANY, VMEM],
        scratch_shapes=[pltpu.VMEM((768, 256), bf16), pltpu.SemaphoreType.DMA((3,))],
        out_shape=[
            pltpu.HBM((768, 256), bf16),
            jax.ShapeDtypeStruct(KEPT, f32),
        ],
        name="second",
        compiler_params=LIMIT,
    )(on_chip(init), summed, on_chip(own), on_chip(other), rates_own, rates_other)

    far_ahead, far_behind, ahead, behind, here = pl.pallas_call(
        apply_first_kernel,
        in_specs=[SCALARS, VMEM, VMEM, VMEM],
        out_specs=[VMEM] * len(FIRST_LEVEL),
        out_shape=[
            (pltpu.HBM if i > 1 else jax.ShapeDtypeStruct)((n, 2, 64, 256), bf16) for i, n in enumerate((3, 2, 2, 3, 1))
        ],
        scratch_shapes=[pltpu.VMEM((ROWS, 2, 64, 256), bf16)],
        name="apply_first",
        compiler_params=LIMIT,
    )(row, on_chip(kept), on_chip(own), on_chip(other))

    def sent(array, step):
        return lax.ppermute(array, "y", [(j, (j + step) % ROWS) for j in range(ROWS)])

    far_ahead = sent(far_ahead, 3)
    far_behind = sent(far_behind, -2)
    ahead = sent(lax.dynamic_update_slice(ahead, far_ahead[2:], (1, 0, 0, 0)), 1)
    behind = lax.dynamic_update_slice(behind, far_ahead[:1], (1, 0, 0, 0))
    behind = sent(lax.dynamic_update_slice(behind, far_behind[:1], (2, 0, 0, 0)), -1)

    total = scattered(second)
    summed = gathered(total)
    result = pl.pallas_call(
        last_kernel,
        in_specs=[SCALARS] + [VMEM] * 4,
        out_specs=ANY,
        out_shape=pltpu.HBM((ROWS, 2, 64, 256), bf16),
        scratch_shapes=[pltpu.VMEM((2, ROWS, 64, 256), bf16), pltpu.SemaphoreType.DMA((2,))],
        name="apply_second",
        compiler_params=LIMIT,
    )(at, on_chip(kept), summed, on_chip(own), on_chip(other))
    parts = exchange(result.reshape(16, 64, 256), ("y", "c"))
    got = [off_chip(here)] + [on_chip(a) for a in (far_ahead, far_behind, ahead, behind)]
    halves = pl.pallas_call(
        collect_kernel,
        in_specs=[VMEM] * 5,
        out_specs=VMEM,
        out_shape=jax.ShapeDtypeStruct((ROWS, 64, 256), bf16),
        name="collect",
        compiler_params=LIMIT,
    )(*got)
    halves = swapped(halves)
    out = pl.pallas_call(
        assemble_first_kernel,
        grid=(1,),
        in_specs=[SCALARS] * 2 + [VMEM] * 6,
        out_specs=pl.BlockSpec((1, 64, 4096), lambda i: (0, 0, 0)),
        out_shape=jax.ShapeDtypeStruct((2, 64, 4096), bf16),
        name="assemble_first",
        compiler_params=LIMIT,
    )(at, row, *got, on_chip(halves))
    return pl.pallas_call(
        assemble_second_kernel,
        grid=(2,),
        in_specs=[VMEM, ANY],
        out_specs=pl.BlockSpec((1, 32, 4096), lambda i: (1, i, 0)),
        out_shape=jax.ShapeDtypeStruct((2, 64, 4096), bf16),
        input_output_aliases={1: 0},
        name="assemble_second",
        compiler_params=LIMIT,
    )(on_chip(parts), out)


def solution(mesh):
    fine = Mesh(mesh.devices.reshape(4, 8, 2, 8), ("x", "z", "c", "y"))
    seq = ("x", "z", "c")
    return jax.shard_map(
        program,
        mesh=fine,
        in_specs=(
            P(None, seq, "y"),
            P(None, seq, "y"),
            P(None, seq, "y"),
            P(None, None, "y", seq),
            P(None, "y", None, None),
        ),
        out_specs=P(None, (*seq, "y"), None),
        check_vma=False,
    )
```

```python
import jax
import jax.numpy as jnp
from jax import lax
from jax.experimental import pallas as pl
from jax.experimental.pallas import tpu as pltpu
from jax.sharding import Mesh, PartitionSpec as P


step_size = 0.05
eps_grad = 1e-05
eps_row = 1e-06
f32 = jnp.float32
bf16 = jnp.bfloat16
NT = (((1,), (1,)), ((), ()))
NN = (((1,), (0,)), ((), ()))
ROWS = 8


def dot(a, b, dims):
    return lax.dot_general(a, b, dims, preferred_element_type=f32)


def row_mean(w, i):
    return jnp.mean(w * w, axis=1 if i == 2 else 0, keepdims=True)


def gradients(keys, values, rate_gate, rate_up, rate_down, w_gate, w_up, w_down):
    gate = dot(w_gate, keys, NT)
    up = dot(w_up, keys, NT)
    err = dot(w_down, values, NT)
    sig = jax.nn.sigmoid(gate)
    silu = gate * sig
    hidden = (silu * up).astype(bf16)
    scaled = (hidden.astype(f32) * rate_down).astype(bf16)
    gate_grad = err * up * sig * (1.0 + gate * (1.0 - sig))
    gate_scaled = (gate_grad * rate_gate).astype(bf16)
    up_scaled = (err * silu * rate_up).astype(bf16)
    return (
        dot(gate_scaled, keys, NN),
        dot(up_scaled, keys, NN),
        dot(scaled, values, NN),
    )


def updated(state, targets, grad_ref):
    result = []
    for i in range(3):
        grad = grad_ref[256 * i : 256 * (i + 1), :].astype(f32)
        rms = jnp.sqrt(jnp.mean(grad * grad, keepdims=True) + eps_grad)
        stepped = state[i] + grad * (step_size / rms)
        result.append(stepped * (targets[i] * lax.rsqrt(row_mean(stepped, i) + eps_row)))
    return result


def first_kernel(at, init_ref, k_ref, v_ref, rates_ref, other_ref, own_ref):
    for head, out_ref in ((1 - at[0], other_ref), (at[0], own_ref)):
        cols = pl.ds(pl.multiple_of(head * 256, 256), 256)
        rates = [rates_ref[i, 0, pl.ds(head, 1), :] for i in range(3)]
        weights = [
            jnp.transpose(init_ref[0, head]),
            jnp.transpose(init_ref[1, head]),
            init_ref[2, head],
        ]
        grads = gradients(k_ref[0, :, cols], v_ref[0, :, cols], *rates, *weights)
        for i in range(3):
            out_ref[256 * i : 256 * (i + 1), :] = grads[i].astype(out_ref.dtype)


KEPT = (1032, 256)


def second_kernel(init_ref, grad_ref, own_ref, other_ref, rates_own_ref, rates_other_ref, out_ref, kept_ref):
    init = [init_ref[i].astype(f32) for i in range(3)]
    targets = [jnp.sqrt(row_mean(w, i)) for i, w in enumerate(init)]
    state = updated(init, targets, grad_ref)
    weights = [w.astype(bf16) for w in state]
    for i in range(3):
        kept_ref[256 * i : 256 * (i + 1), :] = state[i]
    kept_ref[768:1024, :] = jnp.broadcast_to(targets[2], (256, 256))
    kept_ref[1024:1025, :] = targets[0]
    kept_ref[1025:1026, :] = targets[1]
    kept_ref[1026:1032, :] = jnp.zeros((6, 256), f32)
    own = gradients(own_ref[0], own_ref[1], *[rates_own_ref[i : i + 1, :] for i in range(3)], *weights)
    other = gradients(other_ref[0], other_ref[1], *[rates_other_ref[i : i + 1, :] for i in range(3)], *weights)
    for i in range(3):
        out_ref[256 * i : 256 * (i + 1), :] = (own[i] + other[i]).astype(bf16)


def state_of(kept_ref):
    return [kept_ref[256 * i : 256 * (i + 1), :] for i in range(3)]


def applied(q, weights):
    gate = dot(q, weights[0], NT)
    up = dot(q, weights[1], NT)
    hidden = (gate * jax.nn.sigmoid(gate) * up).astype(bf16)
    return dot(hidden, weights[2], NN).astype(bf16)


def prepare_kernel(core_ref, k_ref, v_ref, q_ref, init_ref, rates_ref, own_ref, other_ref, w_ref, rates_own_ref, rates_other_ref):
    for head, out_ref, rates_out_ref in (
        (core_ref[0], own_ref, rates_own_ref),
        (1 - core_ref[0], other_ref, rates_other_ref),
    ):
        cols = pl.ds(pl.multiple_of(head * 256, 256), 256)
        out_ref[0] = k_ref[0, :, cols]
        out_ref[1] = v_ref[0, :, cols]
        out_ref[2] = q_ref[1, :, cols]
        out_ref[3] = q_ref[0, :, cols]
        for i in range(3):
            rates_out_ref[i : i + 1, :] = rates_ref[i, 1, pl.ds(head, 1), :]
    for i in range(3):
        w = init_ref[i, core_ref[0]]
        w_ref[i] = w if i == 2 else jnp.transpose(w)


FIRST_LEVEL = ((2, 3, 4), (-3, -2), (1,), (-1,), (0,))
SOURCES = (0, -3, 2, -1, -4, 1, -2, 3)


def apply_first_kernel(row_ref, kept_ref, own_ref, other_ref, *refs):
    outs, scratch = refs[:-1], refs[-1]
    weights = [w.astype(bf16) for w in state_of(kept_ref)]
    for q, side in ((own_ref[3], 0), (other_ref[3], 1)):
        scratch[:, side] = applied(q, weights).reshape(ROWS, 64, 256)
    for ahead, out_ref in zip(FIRST_LEVEL, outs):
        for i, d in enumerate(ahead):
            out_ref[i] = scratch[lax.rem(row_ref[0] + ROWS + d, ROWS)]


def last_kernel(at, kept_ref, grad_ref, own_ref, other_ref, out_ref):
    targets = [kept_ref[1024:1025, :], kept_ref[1025:1026, :], kept_ref[768:1024, :]]
    state = updated(state_of(kept_ref), targets, grad_ref)
    weights = [w.astype(bf16) for w in state]
    for q, core in ((own_ref[2], at[0]), (other_ref[2], 1 - at[0])):
        out_ref[core] = applied(q, weights).reshape(ROWS, 64, 256)


def total_with_rates_kernel(parts_ref, rates_ref, out_ref, rates_out_ref):
    rates_out_ref[...] = rates_ref[...]
    total_kernel(parts_ref, out_ref)


def total_kernel(parts_ref, out_ref):
    total = jnp.sum(parts_ref[...].astype(f32), axis=0, keepdims=True)
    out_ref[...] = jnp.broadcast_to(total.astype(bf16), out_ref.shape)


def pieces_of(here_ref, far_ahead_ref, far_behind_ref, ahead_ref, behind_ref, side):
    return (
        here_ref[0, side],
        far_ahead_ref[1, side],
        far_behind_ref[1, side],
        ahead_ref[0, side],
        ahead_ref[1, side],
        behind_ref[0, side],
        behind_ref[1, side],
        behind_ref[2, side],
    )


def collect_kernel(*refs):
    for i, piece in enumerate(pieces_of(*refs[:5], 1)):
        refs[5][i] = piece


def assemble_first_kernel(core_ref, row_ref, *refs):
    swapped_ref, out_ref = refs[5], refs[6]
    for i, (source, piece) in enumerate(zip(SOURCES, pieces_of(*refs[:5], 0))):
        first = lax.rem(row_ref[0] + ROWS + source, ROWS) * 512
        own = pl.multiple_of(first + core_ref[0] * 256, 256)
        other = pl.multiple_of(first + (1 - core_ref[0]) * 256, 256)
        out_ref[0, :, pl.ds(own, 256)] = piece
        out_ref[0, :, pl.ds(other, 256)] = swapped_ref[i]


def assemble_second_kernel(parts_ref, prev_ref, out_ref):
    rows = pl.ds(pl.program_id(0) * 32, 32)
    for head in range(16):
        out_ref[0, :, 256 * head : 256 * (head + 1)] = parts_ref[ROWS * (head % 2) + head // 2, rows]


def whole(shape):
    return pl.BlockSpec(shape, lambda i, at: (0,) * len(shape))


def on_chip(array):
    return pltpu.with_memory_space_constraint(array, pltpu.VMEM)


def off_chip(array):
    return pltpu.with_memory_space_constraint(array, pltpu.HBM)


VMEM = pl.BlockSpec(memory_space=pltpu.VMEM)
LIMIT = pltpu.CompilerParams(vmem_limit_bytes=12 << 20)
ANY = pl.BlockSpec(memory_space=pl.ANY)
SCALARS = pl.BlockSpec(memory_space=pltpu.SMEM)


def call(kernel, in_specs, outs, out_specs=None, aliases=None):
    specs = out_specs or [whole(shape) for shape, _ in outs]
    shapes = [jax.ShapeDtypeStruct(shape, dtype) for shape, dtype in outs]
    if len(outs) == 1:
        specs, shapes = specs[0], shapes[0]
    return pl.pallas_call(
        kernel,
        grid_spec=pltpu.PrefetchScalarGridSpec(
            num_scalar_prefetch=1, grid=(1,), in_specs=in_specs, out_specs=specs
        ),
        out_shape=shapes,
        input_output_aliases=aliases or {},
        compiler_params=LIMIT,
    )


def exchange(array, axes):
    return lax.all_to_all(array, axes, split_axis=0, concat_axis=0, tiled=True)


def scattered(partial, rates=None):
    parts = exchange(partial.reshape(32, 24, 256), ("z", "x"))
    args = [on_chip(parts)] if rates is None else [on_chip(parts), on_chip(rates)]
    shapes = [jax.ShapeDtypeStruct((32, 24, 256), bf16), jax.ShapeDtypeStruct((3, 512), f32)][: len(args)]
    result = pl.pallas_call(
        total_kernel if rates is None else total_with_rates_kernel,
        in_specs=[VMEM] * len(args),
        out_specs=[VMEM] * len(args),
        out_shape=shapes,
        name="total",
        compiler_params=LIMIT,
    )(*args)
    return result[0] if rates is None else result


def gathered(total):
    full = exchange(total, ("z", "x"))
    return on_chip(full.reshape(768, 256))


def swapped(array):
    return lax.ppermute(array, "c", [(0, 1), (1, 0)])


def program(query_tokens, key_tokens, value_tokens, token_rates, fast_init):
    core = lax.axis_index("c").astype(jnp.int32)
    at = core.reshape(1)
    row = lax.axis_index("y").astype(jnp.int32).reshape(1)

    first_other, first_own = call(
        first_kernel,
        [
            whole((3, 2, 256, 256)),
            pl.BlockSpec((1, 512, 512), lambda i, at: (0, 0, 0)),
            pl.BlockSpec((1, 512, 512), lambda i, at: (0, 0, 0)),
            whole((3, 2, 2, 512)),
        ],
        [((768, 256), bf16), ((768, 256), f32)],
    )(at, *[off_chip(a) for a in (fast_init, key_tokens, value_tokens, token_rates)])
    first_got = swapped(first_other)
    first = (first_own + first_got.astype(f32)).astype(bf16)
    first, query_tokens, key_tokens, value_tokens, token_rates, fast_init = lax.optimization_barrier(
        (first, query_tokens, key_tokens, value_tokens, token_rates, fast_init)
    )

    tokens = (4, 512, 256)
    own, other, init, rates_own, rates_other = call(
        prepare_kernel,
        [
            pl.BlockSpec((1, 512, 512), lambda i, at: (1, 0, 0)),
            pl.BlockSpec((1, 512, 512), lambda i, at: (1, 0, 0)),
            whole((2, 512, 512)),
            whole((3, 2, 256, 256)),
            whole((3, 2, 2, 512)),
        ],
        [(tokens, bf16), (tokens, bf16), ((3, 256, 256), bf16), ((3, 512), f32), ((3, 512), f32)],
    )(at, *[off_chip(a) for a in (key_tokens, value_tokens, query_tokens, fast_init, token_rates)])
    other = swapped(other)
    rates_other = swapped(rates_other)

    total, rates_other = scattered(first, rates_other)
    total, other, rates_other, own, rates_own, init = lax.optimization_barrier(
        (total, other, rates_other, own, rates_own, init)
    )
    summed = gathered(total)
    second, kept = pl.pallas_call(
        second_kernel,
        in_specs=[VMEM] * 6,
        out_specs=[VMEM] * 2,
        out_shape=[
            pltpu.HBM((768, 256), bf16),
            jax.ShapeDtypeStruct(KEPT, f32),
        ],
        name="second",
        compiler_params=LIMIT,
    )(on_chip(init), summed, on_chip(own), on_chip(other), rates_own, rates_other)

    far_ahead, far_behind, ahead, behind, here = pl.pallas_call(
        apply_first_kernel,
        in_specs=[SCALARS, VMEM, VMEM, VMEM],
        out_specs=[VMEM] * len(FIRST_LEVEL),
        out_shape=[
            (pltpu.HBM if i > 1 else jax.ShapeDtypeStruct)((n, 2, 64, 256), bf16) for i, n in enumerate((3, 2, 2, 3, 1))
        ],
        scratch_shapes=[pltpu.VMEM((ROWS, 2, 64, 256), bf16)],
        name="apply_first",
        compiler_params=LIMIT,
    )(row, on_chip(kept), on_chip(own), on_chip(other))

    def sent(array, step):
        return lax.ppermute(array, "y", [(j, (j + step) % ROWS) for j in range(ROWS)])

    far_ahead = sent(far_ahead, 3)
    far_behind = sent(far_behind, -2)
    ahead = sent(lax.dynamic_update_slice(ahead, far_ahead[2:], (1, 0, 0, 0)), 1)
    behind = lax.dynamic_update_slice(behind, far_ahead[:1], (1, 0, 0, 0))
    behind = sent(lax.dynamic_update_slice(behind, far_behind[:1], (2, 0, 0, 0)), -1)

    total = scattered(second)
    summed = gathered(total)
    result = call(
        last_kernel, [VMEM, VMEM, VMEM, VMEM], [((2, ROWS, 64, 256), bf16)]
    )(at, on_chip(kept), summed, on_chip(own), on_chip(other))
    parts = exchange(result.reshape(16, 64, 256), ("c", "y"))
    got = [off_chip(here)] + [on_chip(a) for a in (far_ahead, far_behind, ahead, behind)]
    halves = pl.pallas_call(
        collect_kernel,
        in_specs=[VMEM] * 5,
        out_specs=VMEM,
        out_shape=jax.ShapeDtypeStruct((ROWS, 64, 256), bf16),
        name="collect",
        compiler_params=LIMIT,
    )(*got)
    halves = swapped(halves)
    out = pl.pallas_call(
        assemble_first_kernel,
        grid=(1,),
        in_specs=[SCALARS] * 2 + [VMEM] * 6,
        out_specs=pl.BlockSpec((1, 64, 4096), lambda i: (0, 0, 0)),
        out_shape=jax.ShapeDtypeStruct((2, 64, 4096), bf16),
        name="assemble_first",
        compiler_params=LIMIT,
    )(at, row, *got, on_chip(halves))
    return pl.pallas_call(
        assemble_second_kernel,
        grid=(2,),
        in_specs=[VMEM, ANY],
        out_specs=pl.BlockSpec((1, 32, 4096), lambda i: (1, i, 0)),
        out_shape=jax.ShapeDtypeStruct((2, 64, 4096), bf16),
        input_output_aliases={1: 0},
        name="assemble_second",
        compiler_params=LIMIT,
    )(on_chip(parts), out)


def solution(mesh):
    fine = Mesh(mesh.devices.reshape(4, 8, 2, 8), ("x", "z", "c", "y"))
    seq = ("x", "z", "c")
    return jax.shard_map(
        program,
        mesh=fine,
        in_specs=(
            P(None, seq, "y"),
            P(None, seq, "y"),
            P(None, seq, "y"),
            P(None, None, "y", seq),
            P(None, "y", None, None),
        ),
        out_specs=P(None, (*seq, "y"), None),
        check_vma=False,
    )
```
